256 devices in a mesh: row: 16 (over y, x), col: 16 (over z, core).
Axes of the slice: x: 4, y: 4, z: 8, core: 2. Of those that a mesh axis runs over, the one named last changes fastest.
Arguments:
- diag_inv: float32 [2, 2048, 2048], P(None, 'col', 'row'), may hold values from -0.125 to 0.125
- cross_block: float32 [2048, 2048], P('row', 'col'), may hold values from -0.125 to 0.125
- coupling: float32 [2, 2048, 65536], P(None, 'row', 'col'), may hold values from -0.125 to 0.125
- panel_loads: float32 [2, 1024, 2048], P(None, 'row', 'col'), may hold values from -6 to 6
- rest_loads: float32 [1024, 65536], P('row', 'col'), may hold values from -6 to 6
Outputs:
- solved: float32 [2, 1024, 2048], P(None, None, 'row')
- rest_updated: float32 [1024, 65536], P('row', 'col')
The draws below stay inside these ranges and needn't reach their ends.
All inputs are finite; a program needn't handle non-finite values.
Results may differ from the reference program's by a relative error of at most 0.00008.
Values sent between devices are 32-bit elements; how exact they have to be, the bound alone decides.
A program may use at most 128 MiB of HBM per device.

```python
import jax
import jax.numpy as jnp
from jax import lax

PANEL = 2048
LOADS = 1024
REST = 65536


def level_of(own_key, extent, pieces, smallest, largest):
    loudness = 1.0
    for dim, parts in pieces:
        steps = jax.random.uniform(jax.random.fold_in(jax.random.fold_in(own_key, 6), dim), (parts,), jnp.float32, smallest / len(pieces), largest / len(pieces))
        loudness = loudness * jnp.repeat(jnp.exp(steps), extent[dim] // parts).reshape((-1,) + (1,) * (len(extent) - 1 - dim))
    return loudness


def normal_values(key, dims, scale, bound, split=(), held_as=jnp.bfloat16):
    array = jax.random.normal(key, dims, jnp.float32) * scale
    if len(split) > 0:
        array = level_of(key, dims, split, -0.22, 0.18) * array
    return jnp.clip(array, min=-bound, max=bound).astype(held_as)


def setup_inputs(seed: int = 0) -> dict:
    key_of = jax.random.split(jax.random.key(seed), 6)
    return {
        "diag_inv": normal_values(key_of[0], (2, PANEL, PANEL), PANEL ** -0.5, 0.125, ((1, 16), (2, 16)), jnp.float32),
        "cross_block": normal_values(key_of[1], (PANEL, PANEL), PANEL ** -0.5, 0.125, ((0, 16), (1, 16)), jnp.float32),
        "coupling": normal_values(key_of[2], (2, PANEL, REST), PANEL ** -0.5, 0.125, ((1, 16), (2, 16)), jnp.float32),
        "panel_loads": normal_values(key_of[3], (2, LOADS, PANEL), 1.0, 6.0, ((1, 16), (2, 16)), jnp.float32),
        "rest_loads": normal_values(key_of[4], (LOADS, REST), 1.0, 6.0, ((0, 16), (1, 16)), jnp.float32),
    }


def product(left, right):
    return jnp.dot(left, right, precision=lax.Precision.HIGHEST, preferred_element_type=jnp.float32)


def reference(diag_inv, cross_block, coupling, panel_loads, rest_loads):
    upper_solved = product(panel_loads[1], diag_inv[1])
    lower_loads = panel_loads[0] - product(upper_solved, cross_block)
    lower_solved = product(lower_loads, diag_inv[0])
    rest_updated = rest_loads - product(upper_solved, coupling[1]) - product(lower_solved, coupling[0])
    return jnp.stack([lower_solved, upper_solved]), rest_updated
```

```python
import functools

import jax
import jax.numpy as jnp
from jax import lax
from jax.experimental import pallas as pl
from jax.experimental.pallas import tpu as pltpu
from jax.sharding import PartitionSpec as P

MESH = pl.DeviceIdType.MESH


def halves(value):
    high = value.astype(jnp.bfloat16)
    low = (value - high.astype(jnp.float32)).astype(jnp.bfloat16)
    return high, low


def product(left, right_halves):
    left_high, left_low = halves(left)
    right_high, right_low = right_halves
    dot = functools.partial(jnp.dot, preferred_element_type=jnp.float32)
    return dot(left_high, right_high) + (dot(left_low, right_high) + dot(left_high, right_low))


def chain_kernel(n, diag_ref, cross_ref, loads_ref, solved_ref, gathered, parts, arrived, send_sem, recv_sem):
    row, col = lax.axis_index("row"), lax.axis_index("col")

    barrier = pltpu.get_barrier_semaphore()

    @pl.loop(1, n)
    def _(step):
        pl.semaphore_signal(barrier, inc=1, device_id={"row": lax.rem(row + step, n)}, device_id_type=MESH)
        pl.semaphore_signal(barrier, inc=1, device_id={"col": lax.rem(col + step, n)}, device_id_type=MESH)

    pl.semaphore_wait(barrier, 2 * (n - 1))

    def copy(phase, axis, mine, peer, source, target):
        return pltpu.make_async_remote_copy(
            src_ref=source,
            dst_ref=target,
            send_sem=send_sem.at[phase, peer],
            recv_sem=recv_sem.at[phase, mine],
            device_id={axis: peer},
            device_id_type=MESH,
        )

    def arrive(phase, axis, peer, place):
        copy(phase, axis, peer, peer, place, place).wait_recv()

    def spread(phase, axis, mine, block, slots):
        @pl.loop(1, n)
        def _(step):
            copy(phase, axis, mine, lax.rem(mine + step, n), block, slots.at[mine]).start()

    def multiply(phase, axis, mine, slots, right, part, other_axis, other, landing):
        right_halves = halves(right)

        @pl.loop(0, n)
        def _(step):
            peer = lax.rem(mine + n - step, n)

            @pl.when(step > 0)
            def _():
                arrive(phase, axis, peer, slots.at[peer])

            part[peer] = product(slots[peer], right_halves)

            @pl.when(peer != other)
            def _():
                copy(phase + 1, other_axis, other, peer, part.at[peer], landing.at[other]).start()

    def total(phase, axis, mine, part, landing):
        def add(step, value):
            peer = lax.rem(mine + n - step, n)
            arrive(phase, axis, peer, landing.at[peer])
            return value + landing[peer]

        return lax.fori_loop(1, n, add, part[mine])

    gathered[0, row] = loads_ref[1]
    spread(0, "row", row, gathered.at[0, row], gathered.at[0])
    multiply(0, "row", row, gathered.at[0], diag_ref[1], parts.at[0], "col", col, arrived.at[0])
    solved_ref[1, col] = total(1, "col", col, parts.at[0], arrived.at[0])
    spread(2, "col", col, solved_ref.at[1, col], solved_ref.at[1])
    multiply(2, "col", col, solved_ref.at[1], cross_ref[...], parts.at[1], "row", row, arrived.at[1])
    gathered[1, row] = loads_ref[0] - total(3, "row", row, parts.at[1], arrived.at[1])
    spread(4, "row", row, gathered.at[1, row], gathered.at[1])
    multiply(4, "row", row, gathered.at[1], diag_ref[0], parts.at[2], "col", col, arrived.at[2])
    solved_ref[0, col] = total(5, "col", col, parts.at[2], arrived.at[2])
    spread(6, "col", col, solved_ref.at[0, col], solved_ref.at[0])

    @pl.loop(1, n)
    def _(step):
        peer = lax.rem(col + n - step, n)
        arrive(6, "col", peer, solved_ref.at[0, peer])

    for phase, axis, mine in enumerate_phases(row, col):
        @pl.loop(1, n)
        def _(step):
            peer = lax.rem(mine + step, n)
            block = gathered.at[0, 0]
            copy(phase, axis, mine, peer, block, block).wait_send()


def enumerate_phases(row, col):
    axes = ("row", "col", "col", "row", "row", "col", "col")
    return [(phase, axis, row if axis == "row" else col) for phase, axis in enumerate(axes)]


def solve_panels(n, diag_inv, cross_block, panel_loads):
    _, height, width = panel_loads.shape
    vmem = pl.BlockSpec(memory_space=pltpu.VMEM)
    block = (n, height, width)
    solved = pl.pallas_call(
        functools.partial(chain_kernel, n),
        out_shape=jax.ShapeDtypeStruct((2,) + block, jnp.float32),
        in_specs=[vmem] * 3,
        out_specs=vmem,
        scratch_shapes=[
            pltpu.VMEM((2,) + block, jnp.float32),
            pltpu.VMEM((3,) + block, jnp.float32),
            pltpu.VMEM((3,) + block, jnp.float32),
            pltpu.SemaphoreType.DMA((7, n)),
            pltpu.SemaphoreType.DMA((7, n)),
        ],
        compiler_params=pltpu.CompilerParams(
            collective_id=0, has_side_effects=True, vmem_limit_bytes=24 * 2**20
        ),
    )(diag_inv, cross_block, panel_loads)
    return solved.reshape(2, n * height, width)


def solution(mesh):
    n = mesh.shape["row"]

    def local(diag_inv, cross_block, coupling, panel_loads, rest_loads):
        solved = solve_panels(n, diag_inv, cross_block, panel_loads)
        left = jnp.concatenate([solved[0], solved[1]], axis=1)
        right = coupling.reshape(-1, coupling.shape[2])
        partial_rest = jnp.dot(left, right, precision=lax.Precision.HIGH, preferred_element_type=jnp.float32)
        rest_updated = rest_loads - lax.psum_scatter(partial_rest, "row", scatter_dimension=0, tiled=True)
        return solved, rest_updated

    in_specs = (
        P(None, "col", "row"),
        P("row", "col"),
        P(None, "row", "col"),
        P(None, "row", "col"),
        P("row", "col"),
    )
    out_specs = (P(None, None, "row"), P("row", "col"))
    return jax.shard_map(local, mesh=mesh, in_specs=in_specs, out_specs=out_specs, check_vma=False)
```

```python
import functools
import math

import jax
import jax.numpy as jnp
from jax import lax
from jax.experimental import pallas as pl
from jax.experimental.pallas import tpu as pltpu
from jax.sharding import PartitionSpec as P

MESH = pl.DeviceIdType.MESH


def halves(value):
    high = value.astype(jnp.bfloat16)
    low = (value - high.astype(jnp.float32)).astype(jnp.bfloat16)
    return high, low


def product(left_halves, right_halves):
    left_high, left_low = left_halves
    right_high, right_low = right_halves
    dot = functools.partial(jnp.dot, preferred_element_type=jnp.float32)
    return dot(left_high, right_high) + (dot(left_low, right_high) + dot(left_high, right_low))


def solve_kernel(
    dims,
    diag_hbm, cross_hbm, coupling_hbm, loads_hbm, rest_hbm,
    solved, out,
    diag, cross, loads, rest,
    gathered, part_up, land_up, part_cross, land_cross, lower, part_low, land_low,
    raw_x, raw_y, high_x, low_x, high_y, low_y,
    along_x, along_y, sum_x, land_x, sum_y, land_y, done_x, done_y, tile_x, tile_y,
    local_sem, s_swap, r_swap, s_a, r_a, s_b, r_b, s_c, r_c, s_d, r_d, s_e, r_e, s_f, r_f, s_g, r_g,
    s_px, r_px, s_py, r_py, s_deal, r_deal, s_ux, r_ux, s_uy, r_uy, s_lx, r_lx, s_ly, r_ly,
    s_sx, r_sx, s_sy, r_sy, s_tx, r_tx, s_ty, r_ty, s_out, r_out,
):
    rows, nx, ny, nz, height, width, qx, qy = dims
    half = nx // 2
    row, col = lax.axis_index("row"), lax.axis_index("col")
    y, x = lax.div(row, nx), lax.rem(row, nx)
    z, core = lax.div(col, 2), lax.rem(col, 2)
    parity, slot = lax.rem(row, 2), lax.div(row, 2)
    holder = parity == core
    sibling = 2 * z + 1 - core

    def send(source, target, send_sem, recv_sem, to_row, to_col):
        copy = pltpu.make_async_remote_copy(
            src_ref=source, dst_ref=target, send_sem=send_sem, recv_sem=recv_sem,
            device_id={"row": to_row, "col": to_col}, device_id_type=MESH,
        )
        copy.start()

    def arrive(place, recv_sem):
        pltpu.make_async_remote_copy(
            src_ref=place, dst_ref=place, send_sem=s_swap.at[0], recv_sem=recv_sem,
            device_id={"row": row, "col": sibling}, device_id_type=MESH,
        ).wait_recv()

    def sent(place, send_sem):
        pltpu.make_async_remote_copy(
            src_ref=place, dst_ref=place, send_sem=send_sem, recv_sem=r_swap.at[0],
            device_id={"row": row, "col": sibling}, device_id_type=MESH,
        ).wait_send()

    own_copies = [
        pltpu.make_async_copy(diag_hbm, diag.at[core], local_sem.at[0]),
        pltpu.make_async_copy(cross_hbm, cross.at[core], local_sem.at[1]),
        pltpu.make_async_copy(loads_hbm.at[0], loads.at[core], local_sem.at[2]),
        pltpu.make_async_copy(rest_hbm, rest, local_sem.at[3]),
        pltpu.make_async_copy(
            coupling_hbm.at[:, :, pl.ds(pl.multiple_of(x * qx, qx), qx)], raw_x.at[core, :, x], local_sem.at[4]
        ),
        pltpu.make_async_copy(
            coupling_hbm.at[:, :, pl.ds(pl.multiple_of(nx * qx + y * qy, qy), qy)], raw_y.at[core, :, y], local_sem.at[5]
        ),
    ]
    for copy in own_copies:
        copy.start()
    own_upper = pltpu.make_async_copy(loads_hbm.at[1], gathered.at[slot, core], local_sem.at[6])

    @pl.when(holder)
    def _():
        own_upper.start()

    barrier = pltpu.get_barrier_semaphore()

    @pl.loop(0, rows)
    def _(step):
        peer = lax.rem(row + step, rows)
        pl.semaphore_signal(barrier, inc=1, device_id={"row": peer, "col": sibling}, device_id_type=MESH)

        @pl.when(step > 0)
        def _():
            pl.semaphore_signal(barrier, inc=1, device_id={"row": peer, "col": col}, device_id_type=MESH)

    @pl.loop(1, nz)
    def _(step):
        peer = lax.rem(z + step, nz)
        pl.semaphore_signal(barrier, inc=1, device_id={"row": row, "col": 2 * peer + core}, device_id_type=MESH)

    pl.semaphore_wait(barrier, 2 * rows - 1 + nz - 1)

    send(diag_hbm, diag.at[core], s_swap.at[0], r_swap.at[0], row, sibling)

    @pl.loop(0, rows)
    def _(step):
        @pl.when(jnp.logical_or(step > 0, jnp.logical_not(holder)))
        def _():
            peer = lax.rem(row + step, rows)
            send(loads_hbm.at[1], gathered.at[slot, core], s_a.at[peer], r_a.at[slot, core], peer, 2 * z + parity)

    send(cross_hbm, cross.at[core], s_swap.at[1], r_swap.at[1], row, sibling)
    send(loads_hbm.at[0], loads.at[core], s_swap.at[2], r_swap.at[2], row, sibling)

    def to_z(part, place, step_slot, landing, s_sem, r_sem):
        @pl.when(step_slot != z)
        def _():
            send(place, landing.at[z], s_sem.at[step_slot], r_sem.at[z], row, 2 * step_slot + core)

    def total_z(part, landing, r_sem):
        def add(step, value):
            peer = lax.rem(z + nz - step, nz)
            arrive(landing.at[peer], r_sem.at[peer])
            return value + landing[peer]

        return lax.fori_loop(1, nz, add, part[z])

    def spread_z(panel, s_sem, r_sem):
        @pl.loop(1, nz)
        def _(step):
            peer = lax.rem(z + step, nz)
            place = solved.at[panel, z, core]
            send(place, place, s_sem.at[peer], r_sem.at[z], row, 2 * peer + core)

    own_copies[0].wait()
    arrive(diag.at[1 - core], r_swap.at[0])

    @pl.when(holder)
    def _():
        own_upper.wait()

    upper_diag = halves(diag[:, 1].reshape(2 * width, width))

    @pl.loop(0, nz)
    def _(step):
        block = lax.rem(slot + nz - step, nz)
        for source in (0, 1):
            @pl.when(jnp.logical_not(jnp.logical_and(2 * block + core == row, source == core)))
            def _():
                arrive(gathered.at[block, source], r_a.at[block, source])

        left = jnp.concatenate([gathered[block, 0], gathered[block, 1]], axis=1)
        part_up[block] = product(halves(left), upper_diag)
        to_z(part_up, part_up.at[block], block, land_up, s_b, r_b)

    @pl.loop(1, nx)
    def _(step):
        peer = lax.rem(x + step, nx)
        send(
            coupling_hbm.at[:, :, pl.ds(pl.multiple_of(peer * qx, qx), qx)], raw_x.at[core, :, x],
            s_px.at[peer], r_px.at[x], y * nx + peer, col,
        )

    @pl.loop(1, ny)
    def _(step):
        peer = lax.rem(y + step, ny)
        send(
            coupling_hbm.at[:, :, pl.ds(pl.multiple_of(nx * qx + peer * qy, qy), qy)], raw_y.at[core, :, y],
            s_py.at[peer], r_py.at[y], peer * nx + x, col,
        )

    solved[1, z, core] = total_z(part_up, land_up, r_b)
    spread_z(1, s_c, r_c)

    own_copies[1].wait()
    arrive(cross.at[1 - core], r_swap.at[1])
    cross_halves = halves(jnp.concatenate([cross[0], cross[1]], axis=1))

    @pl.loop(0, nz)
    def _(step):
        block = lax.rem(z + nz - step, nz)

        @pl.when(step > 0)
        def _():
            arrive(solved.at[1, block, core], r_c.at[block])

        upper = solved[1, block, core]
        along_x[1, x, block] = upper
        along_y[1, y, block] = upper
        part_cross[block] = product(halves(upper), cross_halves)
        owner = 2 * block + core

        @pl.when(owner != row)
        def _():
            send(part_cross.at[block], land_cross.at[row], s_d.at[block], r_d.at[row], owner, col)

    own_copies[2].wait()
    arrive(loads.at[1 - core], r_swap.at[2])

    @pl.when(holder)
    def _():
        def add(step, value):
            peer = lax.rem(row + rows - step, rows)
            arrive(land_cross.at[peer], r_d.at[peer])
            return value + land_cross[peer]

        summed = lax.fori_loop(1, rows, add, part_cross[slot])
        lower[slot] = jnp.concatenate([loads[0], loads[1]], axis=1) - summed

        @pl.loop(1, rows)
        def _(step):
            peer = lax.rem(row + step, rows)
            send(lower.at[slot], lower.at[slot], s_e.at[peer], r_e.at[slot], peer, col)

    own_copies[4].wait()
    own_copies[5].wait()

    @pl.loop(1, nx)
    def _(step):
        peer = lax.rem(x + step, nx)
        arrive(raw_x.at[core, :, peer], r_px.at[peer])

    send(raw_x.at[core], raw_x.at[core], s_deal.at[0], r_deal.at[0], row, sibling)

    @pl.loop(1, ny)
    def _(step):
        peer = lax.rem(y + step, ny)
        arrive(raw_y.at[core, :, peer], r_py.at[peer])

    send(raw_y.at[core], raw_y.at[core], s_deal.at[1], r_deal.at[1], row, sibling)

    lower_diag = halves(diag[:, 0].reshape(2 * width, width))

    @pl.loop(0, nz)
    def _(step):
        block = lax.rem(slot + nz - step, nz)

        @pl.when(2 * block + core != row)
        def _():
            arrive(lower.at[block], r_e.at[block])

        part_low[block] = product(halves(lower[block]), lower_diag)
        to_z(part_low, part_low.at[block], block, land_low, s_f, r_f)

    @pl.loop(1, nx)
    def _(step):
        peer = lax.rem(x + step, nx)
        send(along_x.at[1, x], along_x.at[1, x], s_ux.at[peer], r_ux.at[x], y * nx + peer, col)

    @pl.loop(1, ny)
    def _(step):
        peer = lax.rem(y + step, ny)
        send(along_y.at[1, y], along_y.at[1, y], s_uy.at[peer], r_uy.at[y], peer * nx + x, col)

    send(solved.at[1, :, core], solved.at[1, :, core], s_out.at[1], r_out.at[1], row, sibling)

    arrive(raw_x.at[1 - core], r_deal.at[0])
    arrive(raw_y.at[1 - core], r_deal.at[1])

    def split(raw, high, low, groups):
        @pl.loop(0, 4 * groups)
        def _(index):
            owner, panel, group = lax.div(index, 2 * groups), lax.rem(lax.div(index, groups), 2), lax.rem(index, groups)
            start = pl.multiple_of((panel * groups + group) * width, width)
            block_high, block_low = halves(raw[owner, panel, group])
            high[owner, pl.ds(start, width)] = block_high
            low[owner, pl.ds(start, width)] = block_low

    split(raw_x, high_x, low_x, nx)
    split(raw_y, high_y, low_y, ny)

    solved[0, z, core] = total_z(part_low, land_low, r_f)
    spread_z(0, s_g, r_g)

    @pl.loop(0, nz)
    def _(step):
        block = lax.rem(z + nz - step, nz)

        @pl.when(step > 0)
        def _():
            arrive(solved.at[0, block, core], r_g.at[block])

        found = solved[0, block, core]
        along_x[0, x, block] = found
        along_y[0, y, block] = found
        for distance in range(1, nx):
            peer = lax.rem(x + distance, nx)
            place = along_x.at[0, x, block]
            send(place, place, s_lx.at[peer, block], r_lx.at[x, block], y * nx + peer, col)
        for distance in range(1, ny):
            peer = lax.rem(y + distance, ny)
            place = along_y.at[0, y, block]
            send(place, place, s_ly.at[peer, block], r_ly.at[y, block], peer * nx + x, col)

    send(solved.at[0, :, core], solved.at[0, :, core], s_out.at[0], r_out.at[0], row, sibling)

    @pl.loop(1, nx)
    def _(step):
        peer = lax.rem(x + step, nx)
        arrive(along_x.at[1, peer], r_ux.at[peer])

    @pl.loop(1, ny)
    def _(step):
        peer = lax.rem(y + step, ny)
        arrive(along_y.at[1, peer], r_uy.at[peer])

    def tile_over_y(peer):
        start = peer * half
        for distance in range(1, nx):
            source = lax.rem(x + distance, nx)
            for offset in range(half):
                arrive(along_x.at[0, source, start + offset], r_lx.at[source, start + offset])
        left = halves(jnp.concatenate(
            [along_x[panel, group, pl.ds(start, half)].reshape(half * height, width) for panel in (0, 1) for group in range(nx)],
            axis=1,
        ))
        for owner in (0, 1):
            value = product(left, (high_x[owner], low_x[owner]))
            sum_x[peer, :, owner] = value.reshape(half, height, qx)

        @pl.when(peer != y)
        def _():
            send(sum_x.at[peer], land_x.at[y], s_sx.at[peer], r_sx.at[y], peer * nx + x, col)

    def tile_over_x(offset):
        for distance in range(1, ny):
            source = lax.rem(y + distance, ny)
            for group in range(ny):
                arrive(along_y.at[0, source, group * half + offset], r_ly.at[source, group * half + offset])
        for start in range(0, ny, half):
            left = halves(jnp.concatenate(
                [
                    jnp.concatenate([along_y[panel, group, (start + part) * half + offset] for part in range(half)], axis=0)
                    for panel in (0, 1) for group in range(ny)
                ],
                axis=1,
            ))
            for owner in (0, 1):
                value = product(left, (high_y[owner], low_y[owner]))
                sum_y[offset, pl.ds(start, half), owner] = value.reshape(half, height, qy)
        target = 2 * offset + core

        @pl.when(target != x)
        def _():
            send(sum_y.at[offset], land_y.at[x], s_sy.at[offset], r_sy.at[x], y * nx + target, col)

    @pl.loop(0, half)
    def _(step):
        tile_over_y(lax.rem(y + 1 + 2 * step, ny))
        tile_over_x(lax.rem(lax.div(x, 2) + 1 + step, half))
        tile_over_y(lax.rem(y + 2 + 2 * step, ny))

    own_copies[3].wait()

    @pl.loop(1, ny)
    def _(step):
        peer = lax.rem(y + step, ny)
        arrive(land_x.at[peer], r_sx.at[peer])

    for offset in range(half):
        for owner in (0, 1):
            value = sum_x[y, offset, owner]
            for distance in range(1, ny):
                value = value + land_x[lax.rem(y + distance, ny), offset, owner]
            target = 2 * offset + core
            here = jnp.logical_and(target == x, owner == core)
            done_x[offset, owner] = value

            @pl.when(jnp.logical_not(here))
            def _():
                send(
                    done_x.at[offset, owner], tile_x.at[x], s_tx.at[offset, owner], r_tx.at[x],
                    y * nx + target, 2 * z + owner,
                )

    @pl.when(holder)
    def _():
        @pl.loop(1, nx)
        def _(step):
            peer = lax.rem(x + step, nx)
            arrive(land_y.at[peer], r_sy.at[peer])

        for peer in range(ny):
            for owner in (0, 1):
                value = sum_y[lax.div(x, 2), peer, owner]
                for distance in range(1, nx):
                    value = value + land_y[lax.rem(x + distance, nx), peer, owner]
                done_y[peer, owner] = value

                @pl.when(jnp.logical_not(jnp.logical_and(peer == y, owner == core)))
                def _():
                    send(
                        done_y.at[peer, owner], tile_y.at[y], s_ty.at[peer, owner], r_ty.at[y],
                        peer * nx + x, 2 * z + owner,
                    )

        tile_x[x] = done_x[lax.div(x, 2), core]
        tile_y[y] = done_y[y, core]

    for group in range(nx):
        @pl.when(jnp.logical_not(jnp.logical_and(holder, group == x)))
        def _():
            arrive(tile_x.at[group], r_tx.at[group])

        columns = pl.ds(group * qx, qx)
        out[:, columns] = rest[:, columns] - tile_x[group]

    for group in range(ny):
        @pl.when(jnp.logical_not(jnp.logical_and(holder, group == y)))
        def _():
            arrive(tile_y.at[group], r_ty.at[group])

        columns = pl.ds(nx * qx + group * qy, qy)
        out[:, columns] = rest[:, columns] - tile_y[group]

    for panel in (0, 1):
        arrive(solved.at[panel, :, 1 - core], r_out.at[panel])

    sent(diag.at[core], s_swap.at[0])
    sent(cross.at[core], s_swap.at[1])
    sent(loads.at[core], s_swap.at[2])
    for panel in (0, 1):
        sent(solved.at[panel, :, core], s_out.at[panel])
    sent(raw_x.at[core], s_deal.at[0])
    sent(raw_y.at[core], s_deal.at[1])

    @pl.loop(0, rows)
    def _(step):
        @pl.when(jnp.logical_or(step > 0, jnp.logical_not(holder)))
        def _():
            sent(gathered.at[0, 0], s_a.at[lax.rem(row + step, rows)])

        @pl.when(jnp.logical_and(step > 0, holder))
        def _():
            sent(lower.at[0], s_e.at[lax.rem(row + step, rows)])

    @pl.loop(1, nz)
    def _(step):
        peer = lax.rem(z + step, nz)
        sent(part_up.at[0], s_b.at[peer])
        sent(part_up.at[0], s_c.at[peer])
        sent(part_low.at[0], s_f.at[peer])
        sent(part_low.at[0], s_g.at[peer])

    @pl.loop(0, nz)
    def _(block):
        @pl.when(2 * block + core != row)
        def _():
            sent(part_cross.at[0], s_d.at[block])

        for distance in range(1, nx):
            sent(along_x.at[0, 0, 0], s_lx.at[lax.rem(x + distance, nx), block])
        for distance in range(1, ny):
            sent(along_y.at[0, 0, 0], s_ly.at[lax.rem(y + distance, ny), block])

    @pl.loop(1, nx)
    def _(step):
        peer = lax.rem(x + step, nx)
        sent(raw_x.at[core, :, 0], s_px.at[peer])
        sent(along_x.at[1, 0], s_ux.at[peer])

    @pl.loop(1, ny)
    def _(step):
        peer = lax.rem(y + step, ny)
        sent(raw_y.at[core, :, 0], s_py.at[peer])
        sent(along_y.at[1, 0], s_uy.at[peer])
        sent(sum_x.at[0], s_sx.at[peer])

    @pl.loop(0, half)
    def _(offset):
        target = 2 * offset + core

        @pl.when(target != x)
        def _():
            sent(sum_y.at[0], s_sy.at[offset])

        for owner in (0, 1):
            @pl.when(jnp.logical_not(jnp.logical_and(target == x, owner == core)))
            def _():
                sent(done_x.at[0, 0], s_tx.at[offset, owner])

    @pl.when(holder)
    def _():
        @pl.loop(0, ny)
        def _(peer):
            for owner in (0, 1):
                @pl.when(jnp.logical_not(jnp.logical_and(peer == y, owner == core)))
                def _():
                    sent(done_y.at[0, 0], s_ty.at[peer, owner])


def local(mesh, diag_inv, cross_block, coupling, panel_loads, rest_loads):
    rows, cols = mesh.shape["row"], mesh.shape["col"]
    nx = ny = math.isqrt(rows)
    nz, half = cols // 2, math.isqrt(rows) // 2
    _, height, width = panel_loads.shape
    span = rest_loads.shape[1]
    qx, qy = span // 2 // nx, span // 2 // ny
    f32, bf16 = jnp.float32, jnp.bfloat16
    vmem, dma = pltpu.VMEM, lambda *shape: pltpu.SemaphoreType.DMA(shape)
    block = (height, width)
    whole = pl.BlockSpec(memory_space=pltpu.VMEM)
    solved, rest_updated = pl.pallas_call(
        functools.partial(solve_kernel, (rows, nx, ny, nz, height, width, qx, qy)),
        out_shape=(
            jax.ShapeDtypeStruct((2, nz, 2) + block, f32),
            jax.ShapeDtypeStruct((height, span), f32),
        ),
        in_specs=[pl.BlockSpec(memory_space=pl.ANY)] * 5,
        out_specs=(whole, whole),
        scratch_shapes=[
            vmem((2, 2, width, width), f32),
            vmem((2, width, width), f32),
            vmem((2,) + block, f32),
            vmem((height, span), f32),
            vmem((nz, 2) + block, f32),
            vmem((nz,) + block, f32),
            vmem((nz,) + block, f32),
            vmem((nz, height, 2 * width), f32),
            vmem((rows, height, 2 * width), f32),
            vmem((nz, height, 2 * width), f32),
            vmem((nz,) + block, f32),
            vmem((nz,) + block, f32),
            vmem((2, 2, nx, width, qx), f32),
            vmem((2, 2, ny, width, qy), f32),
            vmem((2, 2 * nx * width, qx), bf16),
            vmem((2, 2 * nx * width, qx), bf16),
            vmem((2, 2 * ny * width, qy), bf16),
            vmem((2, 2 * ny * width, qy), bf16),
            vmem((2, nx, nz) + block, f32),
            vmem((2, ny, nz) + block, f32),
            vmem((ny, half, 2, height, qx), f32),
            vmem((ny, half, 2, height, qx), f32),
            vmem((half, ny, 2, height, qy), f32),
            vmem((nx, ny, 2, height, qy), f32),
            vmem((half, 2, height, qx), f32),
            vmem((ny, 2, height, qy), f32),
            vmem((nx, height, qx), f32),
            vmem((ny, height, qy), f32),
            dma(7), dma(3), dma(3),
            dma(rows), dma(nz, 2),
            dma(nz), dma(nz), dma(nz), dma(nz),
            dma(nz), dma(rows), dma(rows), dma(nz),
            dma(nz), dma(nz), dma(nz), dma(nz),
            dma(nx), dma(nx), dma(ny), dma(ny), dma(2), dma(2),
            dma(nx), dma(nx), dma(ny), dma(ny),
            dma(nx, nz), dma(nx, nz), dma(ny, nz), dma(ny, nz),
            dma(ny), dma(ny), dma(half), dma(nx),
            dma(half, 2), dma(nx), dma(ny, 2), dma(ny),
            dma(2), dma(2),
        ],
        compiler_params=pltpu.CompilerParams(
            collective_id=0, has_side_effects=True, vmem_limit_bytes=56 * 2**20
        ),
    )(diag_inv, cross_block, coupling, panel_loads, rest_loads)
    return solved.reshape(2, rows * height, width), rest_updated


def solution(mesh):
    in_specs = (
        P(None, "col", "row"),
        P("row", "col"),
        P(None, "row", "col"),
        P(None, "row", "col"),
        P("row", "col"),
    )
    out_specs = (P(None, None, "row"), P("row", "col"))
    return jax.shard_map(
        functools.partial(local, mesh), mesh=mesh, in_specs=in_specs, out_specs=out_specs, check_vma=False
    )
```

```python
import functools
import math

import jax
import jax.numpy as jnp
from jax import lax
from jax.experimental import pallas as pl
from jax.experimental.pallas import tpu as pltpu
from jax.sharding import PartitionSpec as P

MESH = pl.DeviceIdType.MESH


def halves(value):
    high = value.astype(jnp.bfloat16)
    low = (value - high.astype(jnp.float32)).astype(jnp.bfloat16)
    return high, low


def product(left_halves, right_halves):
    left_high, left_low = left_halves
    right_high, right_low = right_halves
    dot = functools.partial(jnp.dot, preferred_element_type=jnp.float32)
    return dot(left_high, right_high) + (dot(left_low, right_high) + dot(left_high, right_low))


def farthest_first(size):
    return sorted(range(1, size), key=lambda step: -min(step, size - step))


def solve_kernel(
    dims,
    diag_hbm, cross_hbm, coupling_hbm, loads_hbm, rest_hbm,
    solved, out,
    diag, cross, loads, rest,
    gathered, part_up, land_up, part_cross, land_cross, lower, part_low, land_low,
    raw_x, raw_y, high_x, low_x, high_y, low_y,
    along_x, along_y, sum_x, land_x, sum_y, land_y, done_x, done_y, tile_x, tile_y,
    local_sem, s_swap, r_swap, s_a, r_a, s_b, r_b, s_c, r_c, s_d, r_d, s_e, r_e, s_f, r_f, s_g, r_g,
    s_px, r_px, s_py, r_py, s_deal, r_deal, s_lx, r_lx, s_ly, r_ly,
    s_sx, r_sx, s_sy, r_sy, s_tx, r_tx, s_ty, r_ty, s_out, r_out,
):
    rows, nx, ny, nz, height, width, qx, qy = dims
    half, part = nx // 2, height // 2
    x_steps, y_steps, z_steps = farthest_first(nx), farthest_first(ny), farthest_first(nz)
    plane_steps = sorted(
        ((dy, dx) for dy in range(ny) for dx in range(nx) if (dy, dx) != (0, 0)),
        key=lambda step: -min(step[0], ny - step[0]) - min(step[1], nx - step[1]),
    )
    row, col = lax.axis_index("row"), lax.axis_index("col")
    y, x = lax.div(row, nx), lax.rem(row, nx)
    z, core = lax.div(col, 2), lax.rem(col, 2)
    parity, slot = lax.rem(row, 2), lax.div(row, 2)
    holder = parity == core
    sibling = 2 * z + 1 - core

    def beside(step):
        return lax.rem(y + step[0], ny) * nx + lax.rem(x + step[1], nx)

    def send(source, target, send_sem, recv_sem, to_row, to_col):
        copy = pltpu.make_async_remote_copy(
            src_ref=source, dst_ref=target, send_sem=send_sem, recv_sem=recv_sem,
            device_id={"row": to_row, "col": to_col}, device_id_type=MESH,
        )
        copy.start()

    def arrive(place, recv_sem):
        pltpu.make_async_remote_copy(
            src_ref=place, dst_ref=place, send_sem=s_swap.at[0], recv_sem=recv_sem,
            device_id={"row": row, "col": sibling}, device_id_type=MESH,
        ).wait_recv()

    def sent(place, send_sem):
        pltpu.make_async_remote_copy(
            src_ref=place, dst_ref=place, send_sem=send_sem, recv_sem=r_swap.at[0],
            device_id={"row": row, "col": sibling}, device_id_type=MESH,
        ).wait_send()

    own_copies = [
        pltpu.make_async_copy(diag_hbm, diag.at[core], local_sem.at[0]),
        pltpu.make_async_copy(cross_hbm, cross.at[core], local_sem.at[1]),
        pltpu.make_async_copy(loads_hbm.at[0], loads.at[core], local_sem.at[2]),
        pltpu.make_async_copy(rest_hbm, rest, local_sem.at[3]),
        pltpu.make_async_copy(
            coupling_hbm.at[:, :, pl.ds(pl.multiple_of(x * qx, qx), qx)], raw_x.at[core, :, x], local_sem.at[4]
        ),
        pltpu.make_async_copy(
            coupling_hbm.at[:, :, pl.ds(pl.multiple_of(nx * qx + y * qy, qy), qy)], raw_y.at[core, :, y], local_sem.at[5]
        ),
    ]
    for copy in own_copies:
        copy.start()
    own_upper = [
        pltpu.make_async_copy(loads_hbm.at[1, pl.ds(h * part, part)], gathered.at[h, slot, core], local_sem.at[6 + h])
        for h in (0, 1)
    ]

    @pl.when(holder)
    def _():
        for copy in own_upper:
            copy.start()

    barrier = pltpu.get_barrier_semaphore()

    @pl.loop(0, rows)
    def _(step):
        peer = lax.rem(row + step, rows)
        pl.semaphore_signal(barrier, inc=1, device_id={"row": peer, "col": sibling}, device_id_type=MESH)

        @pl.when(step > 0)
        def _():
            pl.semaphore_signal(barrier, inc=1, device_id={"row": peer, "col": col}, device_id_type=MESH)

    @pl.loop(1, nz)
    def _(step):
        peer = lax.rem(z + step, nz)
        pl.semaphore_signal(barrier, inc=1, device_id={"row": row, "col": 2 * peer + core}, device_id_type=MESH)

    pl.semaphore_wait(barrier, 2 * rows - 1 + nz - 1)

    def rows_of(h):
        return pl.ds(h * part, part)

    def scatter_z(h, parts, landing, s_sem, r_sem):
        for step in z_steps:
            peer = lax.rem(z + step, nz)
            send(parts.at[h, peer], landing.at[h, z], s_sem.at[h, peer], r_sem.at[h, z], row, 2 * peer + core)

    def total_z(h, parts, landing, r_sem):
        value = parts[h, z]
        for step in z_steps:
            peer = lax.rem(z + step, nz)
            arrive(landing.at[h, peer], r_sem.at[h, peer])
            value = value + landing[h, peer]
        return value

    def spread_z(h, panel, value, s_sem, r_sem):
        place = solved.at[panel, z, core, rows_of(h)]
        place[...] = value
        for step in z_steps:
            peer = lax.rem(z + step, nz)
            send(place, place, s_sem.at[h, peer], r_sem.at[h, z], row, 2 * peer + core)

    def found_z(h, panel, r_sem):
        for step in z_steps:
            peer = lax.rem(z + step, nz)
            arrive(solved.at[panel, peer, core, rows_of(h)], r_sem.at[h, peer])
        found = solved[panel, :, core, rows_of(h)]
        along_x[panel, x, :, rows_of(h)] = found
        along_y[panel, y, :, rows_of(h)] = found
        return found.reshape(nz * part, width)

    def gather_upper(h):
        source = loads_hbm.at[1, rows_of(h)]
        target = gathered.at[h, slot, core]
        for step in plane_steps:
            peer = beside(step)
            send(source, target, s_a.at[h, peer], r_a.at[h, slot, core], peer, 2 * z + parity)

        @pl.when(jnp.logical_not(holder))
        def _():
            send(source, target, s_a.at[h, row], r_a.at[h, slot, core], row, sibling)

    def multiply_upper(h):
        for block in range(nz):
            for source in (0, 1):
                @pl.when(jnp.logical_not(jnp.logical_and(2 * block + core == row, source == core)))
                def _():
                    arrive(gathered.at[h, block, source], r_a.at[h, block, source])
        left = jnp.concatenate([gathered[h, :, source].reshape(nz * part, width) for source in (0, 1)], axis=1)
        part_up[h] = product(halves(left), upper_diag).reshape(nz, part, width)
        scatter_z(h, part_up, land_up, s_b, r_b)

    def multiply_cross(h):
        upper = found_z(h, 1, r_c)
        part_cross[h] = product(halves(upper), cross_halves).reshape(nz, part, 2 * width)
        for step in range(nz):
            block = lax.rem(slot + nz // 2 + step, nz)
            owner = 2 * block + core

            @pl.when(owner != row)
            def _():
                send(part_cross.at[h, block], land_cross.at[h, row], s_d.at[h, block], r_d.at[h, row], owner, col)

    def reduce_cross(h):
        @pl.when(holder)
        def _():
            value = jnp.concatenate([loads[0, rows_of(h)], loads[1, rows_of(h)]], axis=1) - part_cross[h, slot]
            for step in plane_steps:
                peer = beside(step)
                arrive(land_cross.at[h, peer], r_d.at[h, peer])
                value = value - land_cross[h, peer]
            place = lower.at[h, slot]
            place[...] = value
            for step in plane_steps:
                peer = beside(step)
                send(place, place, s_e.at[h, peer], r_e.at[h, slot], peer, col)

    def multiply_lower(h):
        for block in range(nz):
            @pl.when(2 * block + core != row)
            def _():
                arrive(lower.at[h, block], r_e.at[h, block])
        part_low[h] = product(halves(lower[h].reshape(nz * part, 2 * width)), lower_diag).reshape(nz, part, width)
        scatter_z(h, part_low, land_low, s_f, r_f)

    def forward(h, panel):
        for step in x_steps:
            peer = lax.rem(x + step, nx)
            place = along_x.at[panel, x, :, rows_of(h)]
            send(place, place, s_lx.at[h, panel, peer], r_lx.at[h, panel, x], y * nx + peer, col)
        for step in y_steps:
            peer = lax.rem(y + step, ny)
            place = along_y.at[panel, y, :, rows_of(h)]
            send(place, place, s_ly.at[h, panel, peer], r_ly.at[h, panel, y], peer * nx + x, col)

    def deal(panel):
        for step in x_steps:
            peer = lax.rem(x + step, nx)
            send(
                coupling_hbm.at[panel, :, pl.ds(pl.multiple_of(peer * qx, qx), qx)], raw_x.at[core, panel, x],
                s_px.at[panel, peer], r_px.at[panel, x], y * nx + peer, col,
            )
        for step in y_steps:
            peer = lax.rem(y + step, ny)
            send(
                coupling_hbm.at[panel, :, pl.ds(pl.multiple_of(nx * qx + peer * qy, qy), qy)], raw_y.at[core, panel, y],
                s_py.at[panel, peer], r_py.at[panel, y], peer * nx + x, col,
            )

    def share_dealt(panel):
        for step in x_steps:
            peer = lax.rem(x + step, nx)
            arrive(raw_x.at[core, panel, peer], r_px.at[panel, peer])
        send(raw_x.at[core, panel], raw_x.at[core, panel], s_deal.at[panel, 0], r_deal.at[panel, 0], row, sibling)
        for step in y_steps:
            peer = lax.rem(y + step, ny)
            arrive(raw_y.at[core, panel, peer], r_py.at[panel, peer])
        send(raw_y.at[core, panel], raw_y.at[core, panel], s_deal.at[panel, 1], r_deal.at[panel, 1], row, sibling)

    def split_dealt(panel):
        arrive(raw_x.at[1 - core, panel], r_deal.at[panel, 0])
        arrive(raw_y.at[1 - core, panel], r_deal.at[panel, 1])
        for raw, high, low, groups in ((raw_x, high_x, low_x, nx), (raw_y, high_y, low_y, ny)):
            @pl.loop(0, 2 * groups)
            def _(index):
                owner, group = lax.div(index, groups), lax.rem(index, groups)
                start = pl.multiple_of((panel * groups + group) * width, width)
                block_high, block_low = halves(raw[owner, panel, group])
                high[owner, pl.ds(start, width)] = block_high
                low[owner, pl.ds(start, width)] = block_low

    send(diag_hbm, diag.at[core], s_swap.at[0], r_swap.at[0], row, sibling)
    gather_upper(0)
    gather_upper(1)
    send(cross_hbm, cross.at[core], s_swap.at[1], r_swap.at[1], row, sibling)
    send(loads_hbm.at[0], loads.at[core], s_swap.at[2], r_swap.at[2], row, sibling)

    own_copies[0].wait()
    arrive(diag.at[1 - core], r_swap.at[0])

    @pl.when(holder)
    def _():
        for copy in own_upper:
            copy.wait()

    upper_diag = halves(diag[:, 1].reshape(2 * width, width))
    multiply_upper(0)
    deal(1)
    multiply_upper(1)

    own_copies[1].wait()
    arrive(cross.at[1 - core], r_swap.at[1])
    cross_halves = halves(jnp.concatenate([cross[0], cross[1]], axis=1))
    for h in (0, 1):
        spread_z(h, 1, total_z(h, part_up, land_up, r_b), s_c, r_c)

    own_copies[2].wait()
    arrive(loads.at[1 - core], r_swap.at[2])
    for h in (0, 1):
        multiply_cross(h)
    for h in (0, 1):
        reduce_cross(h)
    deal(0)

    lower_diag = halves(diag[:, 0].reshape(2 * width, width))
    for h in (0, 1):
        multiply_lower(h)

    for h in (0, 1):
        forward(h, 1)
    send(solved.at[1, :, core], solved.at[1, :, core], s_out.at[1], r_out.at[1], row, sibling)

    own_copies[4].wait()
    own_copies[5].wait()
    for h in (0, 1):
        spread_z(h, 0, total_z(h, part_low, land_low, r_f), s_g, r_g)
    share_dealt(1)
    share_dealt(0)
    for h in (0, 1):
        found_z(h, 0, r_g)
        forward(h, 0)
    send(solved.at[0, :, core], solved.at[0, :, core], s_out.at[0], r_out.at[0], row, sibling)
    split_dealt(1)
    split_dealt(0)

    for h in (0, 1):
        for panel in (1, 0):
            for step in x_steps:
                peer = lax.rem(x + step, nx)
                arrive(along_x.at[panel, peer, :, rows_of(h)], r_lx.at[h, panel, peer])
            for step in y_steps:
                peer = lax.rem(y + step, ny)
                arrive(along_y.at[panel, peer, :, rows_of(h)], r_ly.at[h, panel, peer])

    def tile_over_y(peer):
        start = peer * half
        left = halves(jnp.concatenate(
            [along_x[panel, group, pl.ds(start, half)].reshape(half * height, width) for panel in (0, 1) for group in range(nx)],
            axis=1,
        ))
        for owner in (0, 1):
            value = product(left, (high_x[owner], low_x[owner]))
            sum_x[peer, :, owner] = value.reshape(half, height, qx)

        @pl.when(peer != y)
        def _():
            send(sum_x.at[peer], land_x.at[y], s_sx.at[peer], r_sx.at[y], peer * nx + x, col)

    def tile_over_x(offset):
        for start in range(0, ny, half):
            left = halves(jnp.concatenate(
                [
                    jnp.concatenate([along_y[panel, group, (start + part) * half + offset] for part in range(half)], axis=0)
                    for panel in (0, 1) for group in range(ny)
                ],
                axis=1,
            ))
            for owner in (0, 1):
                value = product(left, (high_y[owner], low_y[owner]))
                sum_y[offset, pl.ds(start, half), owner] = value.reshape(half, height, qy)
        target = 2 * offset + core

        @pl.when(target != x)
        def _():
            send(sum_y.at[offset], land_y.at[x], s_sy.at[offset], r_sy.at[x], y * nx + target, col)

    @pl.loop(0, half)
    def _(step):
        tile_over_y(lax.rem(y + half - step, ny))
        tile_over_x(lax.rem(lax.div(x, 2) + 1 + step, half))
        tile_over_y(lax.rem(y + (half + 1) * (1 - step), ny))

    own_copies[3].wait()

    @pl.loop(1, ny)
    def _(step):
        peer = lax.rem(y + step, ny)
        arrive(land_x.at[peer], r_sx.at[peer])

    for offset in range(half):
        for owner in (0, 1):
            value = sum_x[y, offset, owner]
            for distance in range(1, ny):
                value = value + land_x[lax.rem(y + distance, ny), offset, owner]
            target = 2 * offset + core
            here = jnp.logical_and(target == x, owner == core)
            done_x[offset, owner] = value

            @pl.when(jnp.logical_not(here))
            def _():
                send(
                    done_x.at[offset, owner], tile_x.at[x], s_tx.at[offset, owner], r_tx.at[x],
                    y * nx + target, 2 * z + owner,
                )

    @pl.when(holder)
    def _():
        @pl.loop(1, nx)
        def _(step):
            peer = lax.rem(x + step, nx)
            arrive(land_y.at[peer], r_sy.at[peer])

        for peer in range(ny):
            for owner in (0, 1):
                value = sum_y[lax.div(x, 2), peer, owner]
                for distance in range(1, nx):
                    value = value + land_y[lax.rem(x + distance, nx), peer, owner]
                done_y[peer, owner] = value

                @pl.when(jnp.logical_not(jnp.logical_and(peer == y, owner == core)))
                def _():
                    send(
                        done_y.at[peer, owner], tile_y.at[y], s_ty.at[peer, owner], r_ty.at[y],
                        peer * nx + x, 2 * z + owner,
                    )

        tile_x[x] = done_x[lax.div(x, 2), core]
        tile_y[y] = done_y[y, core]

    for group in range(nx):
        @pl.when(jnp.logical_not(jnp.logical_and(holder, group == x)))
        def _():
            arrive(tile_x.at[group], r_tx.at[group])

        columns = pl.ds(group * qx, qx)
        out[:, columns] = rest[:, columns] - tile_x[group]

    for group in range(ny):
        @pl.when(jnp.logical_not(jnp.logical_and(holder, group == y)))
        def _():
            arrive(tile_y.at[group], r_ty.at[group])

        columns = pl.ds(nx * qx + group * qy, qy)
        out[:, columns] = rest[:, columns] - tile_y[group]

    for panel in (0, 1):
        arrive(solved.at[panel, :, 1 - core], r_out.at[panel])

    sent(diag.at[core], s_swap.at[0])
    sent(cross.at[core], s_swap.at[1])
    sent(loads.at[core], s_swap.at[2])
    for panel in (0, 1):
        sent(solved.at[panel, :, core], s_out.at[panel])
    for panel in (0, 1):
        sent(raw_x.at[core, panel], s_deal.at[panel, 0])
        sent(raw_y.at[core, panel], s_deal.at[panel, 1])

    for h in (0, 1):
        @pl.loop(0, rows)
        def _(step):
            peer = lax.rem(row + step, rows)

            @pl.when(jnp.logical_or(step > 0, jnp.logical_not(holder)))
            def _():
                sent(gathered.at[0, 0, 0], s_a.at[h, peer])

            @pl.when(jnp.logical_and(step > 0, holder))
            def _():
                sent(lower.at[0, 0], s_e.at[h, peer])

        @pl.loop(1, nz)
        def _(step):
            peer = lax.rem(z + step, nz)
            for sem in (s_b, s_c, s_f, s_g):
                sent(part_up.at[0, 0], sem.at[h, peer])

        @pl.loop(0, nz)
        def _(block):
            @pl.when(2 * block + core != row)
            def _():
                sent(part_cross.at[0, 0], s_d.at[h, block])

        for panel in (0, 1):
            for step in x_steps:
                sent(along_x.at[0, 0, :, rows_of(0)], s_lx.at[h, panel, lax.rem(x + step, nx)])
            for step in y_steps:
                sent(along_y.at[0, 0, :, rows_of(0)], s_ly.at[h, panel, lax.rem(y + step, ny)])

    @pl.loop(1, nx)
    def _(step):
        peer = lax.rem(x + step, nx)
        for panel in (0, 1):
            sent(raw_x.at[core, panel, 0], s_px.at[panel, peer])

    @pl.loop(1, ny)
    def _(step):
        peer = lax.rem(y + step, ny)
        for panel in (0, 1):
            sent(raw_y.at[core, panel, 0], s_py.at[panel, peer])
        sent(sum_x.at[0], s_sx.at[peer])

    @pl.loop(0, half)
    def _(offset):
        target = 2 * offset + core

        @pl.when(target != x)
        def _():
            sent(sum_y.at[0], s_sy.at[offset])

        for owner in (0, 1):
            @pl.when(jnp.logical_not(jnp.logical_and(target == x, owner == core)))
            def _():
                sent(done_x.at[0, 0], s_tx.at[offset, owner])

    @pl.when(holder)
    def _():
        @pl.loop(0, ny)
        def _(peer):
            for owner in (0, 1):
                @pl.when(jnp.logical_not(jnp.logical_and(peer == y, owner == core)))
                def _():
                    sent(done_y.at[0, 0], s_ty.at[peer, owner])


def local(mesh, diag_inv, cross_block, coupling, panel_loads, rest_loads):
    rows, cols = mesh.shape["row"], mesh.shape["col"]
    nx = ny = math.isqrt(rows)
    nz, half = cols // 2, math.isqrt(rows) // 2
    _, height, width = panel_loads.shape
    span = rest_loads.shape[1]
    qx, qy = span // 2 // nx, span // 2 // ny
    f32, bf16 = jnp.float32, jnp.bfloat16
    vmem, dma = pltpu.VMEM, lambda *shape: pltpu.SemaphoreType.DMA(shape)
    block, piece = (height, width), (height // 2, width)
    whole = pl.BlockSpec(memory_space=pltpu.VMEM)
    solved, rest_updated = pl.pallas_call(
        functools.partial(solve_kernel, (rows, nx, ny, nz, height, width, qx, qy)),
        out_shape=(
            jax.ShapeDtypeStruct((2, nz, 2) + block, f32),
            jax.ShapeDtypeStruct((height, span), f32),
        ),
        in_specs=[pl.BlockSpec(memory_space=pltpu.HBM)] * 5,
        out_specs=(whole, whole),
        scratch_shapes=[
            vmem((2, 2, width, width), f32),
            vmem((2, width, width), f32),
            vmem((2,) + block, f32),
            vmem((height, span), f32),
            vmem((2, nz, 2) + piece, f32),
            vmem((2, nz) + piece, f32),
            vmem((2, nz) + piece, f32),
            vmem((2, nz, height // 2, 2 * width), f32),
            vmem((2, rows, height // 2, 2 * width), f32),
            vmem((2, nz, height // 2, 2 * width), f32),
            vmem((2, nz) + piece, f32),
            vmem((2, nz) + piece, f32),
            vmem((2, 2, nx, width, qx), f32),
            vmem((2, 2, ny, width, qy), f32),
            vmem((2, 2 * nx * width, qx), bf16),
            vmem((2, 2 * nx * width, qx), bf16),
            vmem((2, 2 * ny * width, qy), bf16),
            vmem((2, 2 * ny * width, qy), bf16),
            vmem((2, nx, nz) + block, f32),
            vmem((2, ny, nz) + block, f32),
            vmem((ny, half, 2, height, qx), f32),
            vmem((ny, half, 2, height, qx), f32),
            vmem((half, ny, 2, height, qy), f32),
            vmem((nx, ny, 2, height, qy), f32),
            vmem((half, 2, height, qx), f32),
            vmem((ny, 2, height, qy), f32),
            vmem((nx, height, qx), f32),
            vmem((ny, height, qy), f32),
            dma(8), dma(3), dma(3),
            dma(2, rows), dma(2, nz, 2),
            dma(2, nz), dma(2, nz), dma(2, nz), dma(2, nz),
            dma(2, nz), dma(2, rows), dma(2, rows), dma(2, nz),
            dma(2, nz), dma(2, nz), dma(2, nz), dma(2, nz),
            dma(2, nx), dma(2, nx), dma(2, ny), dma(2, ny), dma(2, 2), dma(2, 2),
            dma(2, 2, nx), dma(2, 2, nx), dma(2, 2, ny), dma(2, 2, ny),
            dma(ny), dma(ny), dma(half), dma(nx),
            dma(half, 2), dma(nx), dma(ny, 2), dma(ny),
            dma(2), dma(2),
        ],
        compiler_params=pltpu.CompilerParams(
            collective_id=0, has_side_effects=True, vmem_limit_bytes=42 * 2**20
        ),
    )(*(pltpu.with_memory_space_constraint(arg, pltpu.HBM) for arg in (diag_inv, cross_block, coupling, panel_loads, rest_loads)))
    return solved.reshape(2, rows * height, width), rest_updated


def solution(mesh):
    in_specs = (
        P(None, "col", "row"),
        P("row", "col"),
        P(None, "row", "col"),
        P(None, "row", "col"),
        P("row", "col"),
    )
    out_specs = (P(None, None, "row"), P("row", "col"))
    return jax.shard_map(
        functools.partial(local, mesh), mesh=mesh, in_specs=in_specs, out_specs=out_specs, check_vma=False
    )
```

```python
import functools
import math

import jax
import jax.numpy as jnp
from jax import lax
from jax.experimental import pallas as pl
from jax.experimental.pallas import tpu as pltpu
from jax.sharding import PartitionSpec as P

MESH = pl.DeviceIdType.MESH


def halves(value):
    high = value.astype(jnp.bfloat16)
    low = (value - high.astype(jnp.float32)).astype(jnp.bfloat16)
    return high, low


def product(left_halves, right_halves):
    left_high, left_low = left_halves
    right_high, right_low = right_halves
    dot = functools.partial(jnp.dot, preferred_element_type=jnp.float32)
    return dot(left_high, right_high) + (dot(left_low, right_high) + dot(left_high, right_low))


def farthest_first(size):
    return sorted(range(1, size), key=lambda step: -min(step, size - step))


def solve_kernel(
    dims,
    diag_hbm, cross_hbm, coupling_hbm, loads_hbm, rest_hbm,
    solved, out,
    diag, cross, loads, rest,
    gathered, part_up, land_up, part_cross, land_cross, lower, part_low, land_low,
    raw_x, raw_y, high_x, low_x, high_y, low_y,
    along_x, along_y, sum_x, land_x, relay_x, sum_y, land_y, relay_y, done_x, done_y, tile_x, tile_y,
    local_sem, s_swap, r_swap, s_a, r_a, s_b, r_b, s_c, r_c, s_d, r_d, s_e, r_e, s_f, r_f, s_g, r_g,
    s_px, r_px, s_py, r_py, s_deal, r_deal, s_lx, r_lx, s_ly, r_ly,
    s_sx, r_sx, s_sy, r_sy, s_rx, r_rx, s_ry, r_ry, s_far, r_far, s_fz, r_fz, s_tx, r_tx, s_ty, r_ty, s_out, r_out,
):
    rows, nx, ny, nz, height, width, qx, qy = dims
    half, part = nx // 2, height // 2
    x_steps, y_steps, z_steps = farthest_first(nx), farthest_first(ny), farthest_first(nz)
    plane_steps = sorted(
        ((dy, dx) for dy in range(ny) for dx in range(nx) if (dy, dx) != (0, 0)),
        key=lambda step: -min(step[0], ny - step[0]) - min(step[1], nx - step[1]),
    )
    row, col = lax.axis_index("row"), lax.axis_index("col")
    y, x = lax.div(row, nx), lax.rem(row, nx)
    z, core = lax.div(col, 2), lax.rem(col, 2)
    parity, slot = lax.rem(row, 2), lax.div(row, 2)
    holder = parity == core
    sibling = 2 * z + 1 - core

    def beside(step):
        return lax.rem(y + step[0], ny) * nx + lax.rem(x + step[1], nx)

    def send(source, target, send_sem, recv_sem, to_row, to_col):
        copy = pltpu.make_async_remote_copy(
            src_ref=source, dst_ref=target, send_sem=send_sem, recv_sem=recv_sem,
            device_id={"row": to_row, "col": to_col}, device_id_type=MESH,
        )
        copy.start()

    def arrive(place, recv_sem):
        pltpu.make_async_remote_copy(
            src_ref=place, dst_ref=place, send_sem=s_swap.at[0], recv_sem=recv_sem,
            device_id={"row": row, "col": sibling}, device_id_type=MESH,
        ).wait_recv()

    def sent(place, send_sem):
        pltpu.make_async_remote_copy(
            src_ref=place, dst_ref=place, send_sem=send_sem, recv_sem=r_swap.at[0],
            device_id={"row": row, "col": sibling}, device_id_type=MESH,
        ).wait_send()

    own_copies = [
        pltpu.make_async_copy(diag_hbm, diag.at[core], local_sem.at[0]),
        pltpu.make_async_copy(cross_hbm, cross.at[core], local_sem.at[1]),
        pltpu.make_async_copy(loads_hbm.at[0], loads.at[core], local_sem.at[2]),
        pltpu.make_async_copy(rest_hbm, rest, local_sem.at[3]),
        pltpu.make_async_copy(
            coupling_hbm.at[:, :, pl.ds(pl.multiple_of(x * qx, qx), qx)], raw_x.at[core, :, x], local_sem.at[4]
        ),
        pltpu.make_async_copy(
            coupling_hbm.at[:, :, pl.ds(pl.multiple_of(nx * qx + y * qy, qy), qy)], raw_y.at[core, :, y], local_sem.at[5]
        ),
    ]
    for copy in own_copies:
        copy.start()
    own_upper = [
        pltpu.make_async_copy(loads_hbm.at[1, pl.ds(h * part, part)], gathered.at[h, slot, core], local_sem.at[6 + h])
        for h in (0, 1)
    ]

    @pl.when(holder)
    def _():
        for copy in own_upper:
            copy.start()

    barrier = pltpu.get_barrier_semaphore()

    @pl.loop(0, rows)
    def _(step):
        peer = lax.rem(row + step, rows)
        pl.semaphore_signal(barrier, inc=1, device_id={"row": peer, "col": sibling}, device_id_type=MESH)

        @pl.when(step > 0)
        def _():
            pl.semaphore_signal(barrier, inc=1, device_id={"row": peer, "col": col}, device_id_type=MESH)

    @pl.loop(1, nz)
    def _(step):
        peer = lax.rem(z + step, nz)
        pl.semaphore_signal(barrier, inc=1, device_id={"row": row, "col": 2 * peer + core}, device_id_type=MESH)

    pl.semaphore_wait(barrier, 2 * rows - 1 + nz - 1)

    def rows_of(h):
        return pl.ds(h * part, part)

    def scatter_z(h, parts, landing, s_sem, r_sem):
        for step in z_steps:
            peer = lax.rem(z + step, nz)
            send(parts.at[h, peer], landing.at[h, z], s_sem.at[h, peer], r_sem.at[h, z], row, 2 * peer + core)

    def total_z(h, parts, landing, r_sem):
        value = parts[h, z]
        for step in z_steps:
            peer = lax.rem(z + step, nz)
            arrive(landing.at[h, peer], r_sem.at[h, peer])
            value = value + landing[h, peer]
        return value

    def spread_z(h, panel, value, s_sem, r_sem):
        place = solved.at[panel, z, core, rows_of(h)]
        place[...] = value
        for step in z_steps:
            peer = lax.rem(z + step, nz)
            send(place, place, s_sem.at[h, peer], r_sem.at[h, z], row, 2 * peer + core)

    def found_z(h, panel, r_sem):
        for step in z_steps:
            peer = lax.rem(z + step, nz)
            arrive(solved.at[panel, peer, core, rows_of(h)], r_sem.at[h, peer])
        found = solved[panel, :, core, rows_of(h)]
        along_x[panel, x, :, rows_of(h)] = found
        along_y[panel, y, :, rows_of(h)] = found
        return found.reshape(nz * part, width)

    def gather_upper(h):
        source = loads_hbm.at[1, rows_of(h)]
        target = gathered.at[h, slot, core]
        for step in plane_steps:
            peer = beside(step)
            send(source, target, s_a.at[h, peer], r_a.at[h, slot, core], peer, 2 * z + parity)

        @pl.when(jnp.logical_not(holder))
        def _():
            send(source, target, s_a.at[h, row], r_a.at[h, slot, core], row, sibling)

    def multiply_upper(h):
        for block in range(nz):
            for source in (0, 1):
                @pl.when(jnp.logical_not(jnp.logical_and(2 * block + core == row, source == core)))
                def _():
                    arrive(gathered.at[h, block, source], r_a.at[h, block, source])
        left = jnp.concatenate([gathered[h, :, source].reshape(nz * part, width) for source in (0, 1)], axis=1)
        part_up[h] = product(halves(left), upper_diag).reshape(nz, part, width)
        scatter_z(h, part_up, land_up, s_b, r_b)

    def multiply_cross(h):
        upper = found_z(h, 1, r_c)
        part_cross[h] = product(halves(upper), cross_halves).reshape(nz, part, 2 * width)
        for step in range(nz):
            block = lax.rem(slot + nz // 2 + step, nz)
            owner = 2 * block + core

            @pl.when(owner != row)
            def _():
                send(part_cross.at[h, block], land_cross.at[h, row], s_d.at[h, block], r_d.at[h, row], owner, col)

    def reduce_cross(h):
        @pl.when(holder)
        def _():
            value = jnp.concatenate([loads[0, rows_of(h)], loads[1, rows_of(h)]], axis=1) - part_cross[h, slot]
            for step in plane_steps:
                peer = beside(step)
                arrive(land_cross.at[h, peer], r_d.at[h, peer])
                value = value - land_cross[h, peer]
            place = lower.at[h, slot]
            place[...] = value
            for step in plane_steps:
                peer = beside(step)
                send(place, place, s_e.at[h, peer], r_e.at[h, slot], peer, col)

    def multiply_lower(h):
        for block in range(nz):
            @pl.when(2 * block + core != row)
            def _():
                arrive(lower.at[h, block], r_e.at[h, block])
        part_low[h] = product(halves(lower[h].reshape(nz * part, 2 * width)), lower_diag).reshape(nz, part, width)
        scatter_z(h, part_low, land_low, s_f, r_f)

    def forward(h, panel):
        for step in x_steps[panel:]:
            peer = lax.rem(x + step, nx)
            place = along_x.at[panel, x, :, rows_of(h)]
            send(place, place, s_lx.at[h, panel, peer], r_lx.at[h, panel, x], y * nx + peer, col)
        for step in y_steps[panel:]:
            peer = lax.rem(y + step, ny)
            place = along_y.at[panel, y, :, rows_of(h)]
            send(place, place, s_ly.at[h, panel, peer], r_ly.at[h, panel, y], peer * nx + x, col)

    def deal(panel):
        for step in x_steps:
            peer = lax.rem(x + step, nx)
            send(
                coupling_hbm.at[panel, :, pl.ds(pl.multiple_of(peer * qx, qx), qx)], raw_x.at[core, panel, x],
                s_px.at[panel, peer], r_px.at[panel, x], y * nx + peer, col,
            )
        for step in y_steps:
            peer = lax.rem(y + step, ny)
            send(
                coupling_hbm.at[panel, :, pl.ds(pl.multiple_of(nx * qx + peer * qy, qy), qy)], raw_y.at[core, panel, y],
                s_py.at[panel, peer], r_py.at[panel, y], peer * nx + x, col,
            )

    def share_dealt(panel):
        for step in x_steps:
            peer = lax.rem(x + step, nx)
            arrive(raw_x.at[core, panel, peer], r_px.at[panel, peer])
        send(raw_x.at[core, panel], raw_x.at[core, panel], s_deal.at[panel, 0], r_deal.at[panel, 0], row, sibling)
        for step in y_steps:
            peer = lax.rem(y + step, ny)
            arrive(raw_y.at[core, panel, peer], r_py.at[panel, peer])
        send(raw_y.at[core, panel], raw_y.at[core, panel], s_deal.at[panel, 1], r_deal.at[panel, 1], row, sibling)

    def split_dealt(panel):
        arrive(raw_x.at[1 - core, panel], r_deal.at[panel, 0])
        arrive(raw_y.at[1 - core, panel], r_deal.at[panel, 1])
        for raw, high, low, groups in ((raw_x, high_x, low_x, nx), (raw_y, high_y, low_y, ny)):
            @pl.loop(0, 2 * groups)
            def _(index):
                owner, group = lax.div(index, groups), lax.rem(index, groups)
                start = pl.multiple_of((panel * groups + group) * width, width)
                block_high, block_low = halves(raw[owner, panel, group])
                high[owner, pl.ds(start, width)] = block_high
                low[owner, pl.ds(start, width)] = block_low

    send(diag_hbm, diag.at[core], s_swap.at[0], r_swap.at[0], row, sibling)
    gather_upper(0)
    gather_upper(1)
    send(cross_hbm, cross.at[core], s_swap.at[1], r_swap.at[1], row, sibling)
    send(loads_hbm.at[0], loads.at[core], s_swap.at[2], r_swap.at[2], row, sibling)

    own_copies[0].wait()
    arrive(diag.at[1 - core], r_swap.at[0])

    @pl.when(holder)
    def _():
        for copy in own_upper:
            copy.wait()

    upper_diag = halves(diag[:, 1].reshape(2 * width, width))
    multiply_upper(0)
    deal(1)
    multiply_upper(1)

    own_copies[1].wait()
    arrive(cross.at[1 - core], r_swap.at[1])
    cross_halves = halves(jnp.concatenate([cross[0], cross[1]], axis=1))
    for h in (0, 1):
        spread_z(h, 1, total_z(h, part_up, land_up, r_b), s_c, r_c)

    x_far, y_far = lax.rem(x + half, nx), lax.rem(y + half, ny)
    own_block = solved.at[1, z, core]
    send(own_block, along_x.at[1, x, z], s_far.at[0], r_far.at[0], y * nx + x_far, col)
    send(own_block, along_y.at[1, y, z], s_far.at[1], r_far.at[1], y_far * nx + x, col)

    own_copies[2].wait()
    arrive(loads.at[1 - core], r_swap.at[2])
    for h in (0, 1):
        multiply_cross(h)
    far_places = (along_x.at[1, x_far], along_y.at[1, y_far])
    for axis in (0, 1):
        place = far_places[axis].at[z]
        arrive(place, r_far.at[axis])
        for step in z_steps:
            peer = lax.rem(z + step, nz)
            send(place, place, s_fz.at[axis, peer], r_fz.at[axis, z], row, 2 * peer + core)
    for h in (0, 1):
        reduce_cross(h)
    deal(0)

    lower_diag = halves(diag[:, 0].reshape(2 * width, width))
    for h in (0, 1):
        multiply_lower(h)

    for h in (0, 1):
        forward(h, 1)
    send(solved.at[1, :, core], solved.at[1, :, core], s_out.at[1], r_out.at[1], row, sibling)

    own_copies[4].wait()
    own_copies[5].wait()
    for h in (0, 1):
        spread_z(h, 0, total_z(h, part_low, land_low, r_f), s_g, r_g)
    share_dealt(1)
    share_dealt(0)
    for h in (0, 1):
        found_z(h, 0, r_g)
        forward(h, 0)
    send(solved.at[0, :, core], solved.at[0, :, core], s_out.at[0], r_out.at[0], row, sibling)
    split_dealt(1)
    split_dealt(0)

    for h in (0, 1):
        for panel in (1, 0):
            for step in x_steps[panel:]:
                peer = lax.rem(x + step, nx)
                arrive(along_x.at[panel, peer, :, rows_of(h)], r_lx.at[h, panel, peer])
            for step in y_steps[panel:]:
                peer = lax.rem(y + step, ny)
                arrive(along_y.at[panel, peer, :, rows_of(h)], r_ly.at[h, panel, peer])

    for axis in (0, 1):
        for step in z_steps:
            peer = lax.rem(z + step, nz)
            arrive(far_places[axis].at[peer], r_fz.at[axis, peer])

    def tile_over_y(peer):
        start = peer * half
        left = halves(jnp.concatenate(
            [along_x[panel, group, pl.ds(start, half)].reshape(half * height, width) for panel in (0, 1) for group in range(nx)],
            axis=1,
        ))
        for owner in (0, 1):
            value = product(left, (high_x[owner], low_x[owner]))
            sum_x[peer, :, owner] = value.reshape(half, height, qx)

    def tile_over_x(offset):
        for start in range(0, ny, half):
            left = halves(jnp.concatenate(
                [
                    jnp.concatenate([along_y[panel, group, (start + part) * half + offset] for part in range(half)], axis=0)
                    for panel in (0, 1) for group in range(ny)
                ],
                axis=1,
            ))
            for owner in (0, 1):
                value = product(left, (high_y[owner], low_y[owner]))
                sum_y[offset, pl.ds(start, half), owner] = value.reshape(half, height, qy)
    y_up, y_down = lax.rem(y + 1, ny), lax.rem(y + ny - 1, ny)
    x_up, x_down = lax.rem(x + 1, nx), lax.rem(x + nx - 1, nx)
    row_up, row_down = y_up * nx + x, y_down * nx + x
    side_up, side_down = y * nx + x_up, y * nx + x_down
    own_offset = lax.div(x, 2)
    up_offset, down_offset = lax.div(x_up, 2), lax.div(x_down, 2)
    first, last = pl.ds(0, half), pl.ds(half, half)

    @pl.loop(0, 2)
    def _(step):
        tile_over_y(jnp.where(step == 0, y_far, y_down))

        @pl.when(step == 0)
        def _():
            send(sum_x.at[y_far, 0], relay_x.at[0], s_rx.at[0], r_rx.at[0], row_up, col)
            send(sum_x.at[y_far, 1], relay_x.at[1], s_rx.at[1], r_rx.at[1], row_down, col)

        @pl.when(step == 1)
        def _():
            send(sum_x.at[y_down, 0], land_x.at[1, 0], s_sx.at[1, 0], r_sx.at[1, 0], row_down, col)

        tile_over_x(jnp.where(
            step == 0, jnp.where(holder, 1 - own_offset, up_offset), jnp.where(holder, own_offset, down_offset)
        ))

        @pl.when(jnp.logical_and(step == 0, holder))
        def _():
            send(sum_y.at[1 - own_offset, first], relay_y.at[0], s_ry.at[0], r_ry.at[0], side_up, col)
            send(sum_y.at[1 - own_offset, last], relay_y.at[1], s_ry.at[1], r_ry.at[1], side_down, col)

        @pl.when(jnp.logical_and(step == 0, jnp.logical_not(holder)))
        def _():
            send(sum_y.at[up_offset, last], land_y.at[0, last], s_sy.at[0, 1], r_sy.at[0, 1], side_up, col)

        @pl.when(jnp.logical_and(step == 1, jnp.logical_not(holder)))
        def _():
            send(sum_y.at[down_offset, first], land_y.at[1, first], s_sy.at[1, 0], r_sy.at[1, 0], side_down, col)

        @pl.when(step == 1)
        def _():
            arrive(relay_x.at[0], r_rx.at[0])
            sum_x[y_up, 0] = sum_x[y_up, 0] + relay_x[0]
            send(sum_x.at[y_up, 0], land_x.at[0, 0], s_sx.at[0, 0], r_sx.at[0, 0], row_up, col)
            arrive(relay_x.at[1], r_rx.at[1])
            sum_x[y_down, 1] = sum_x[y_down, 1] + relay_x[1]
            send(sum_x.at[y_down, 1], land_x.at[1, 1], s_sx.at[1, 1], r_sx.at[1, 1], row_down, col)

            @pl.when(jnp.logical_not(holder))
            def _():
                arrive(relay_y.at[0], r_ry.at[0])
                sum_y[up_offset, first] = sum_y[up_offset, first] + relay_y[0]
                send(sum_y.at[up_offset, first], land_y.at[0, first], s_sy.at[0, 0], r_sy.at[0, 0], side_up, col)
                arrive(relay_y.at[1], r_ry.at[1])
                sum_y[down_offset, last] = sum_y[down_offset, last] + relay_y[1]
                send(sum_y.at[down_offset, last], land_y.at[1, last], s_sy.at[1, 1], r_sy.at[1, 1], side_down, col)

        tile_over_y(jnp.where(step == 0, y_up, y))

        @pl.when(step == 0)
        def _():
            send(sum_x.at[y_up, 1], land_x.at[0, 1], s_sx.at[0, 1], r_sx.at[0, 1], row_up, col)

    own_copies[3].wait()

    for offset in range(half):
        for side in (0, 1):
            arrive(land_x.at[side, offset], r_sx.at[side, offset])
        for owner in (0, 1):
            value = sum_x[y, offset, owner] + land_x[0, offset, owner] + land_x[1, offset, owner]
            target = 2 * offset + core
            here = jnp.logical_and(target == x, owner == core)
            done_x[offset, owner] = value

            @pl.when(jnp.logical_not(here))
            def _():
                send(
                    done_x.at[offset, owner], tile_x.at[x], s_tx.at[offset, owner], r_tx.at[x],
                    y * nx + target, 2 * z + owner,
                )

    @pl.when(holder)
    def _():
        for peer in range(ny):
            if peer % half == 0:
                for side in (0, 1):
                    arrive(land_y.at[side, pl.ds(peer, half)], r_sy.at[side, peer // half])
            for owner in (0, 1):
                value = sum_y[own_offset, peer, owner] + land_y[0, peer, owner] + land_y[1, peer, owner]
                done_y[peer, owner] = value

                @pl.when(jnp.logical_not(jnp.logical_and(peer == y, owner == core)))
                def _():
                    send(
                        done_y.at[peer, owner], tile_y.at[y], s_ty.at[peer, owner], r_ty.at[y],
                        peer * nx + x, 2 * z + owner,
                    )

        tile_x[x] = done_x[lax.div(x, 2), core]
        tile_y[y] = done_y[y, core]

    for group in range(nx):
        @pl.when(jnp.logical_not(jnp.logical_and(holder, group == x)))
        def _():
            arrive(tile_x.at[group], r_tx.at[group])

        columns = pl.ds(group * qx, qx)
        out[:, columns] = rest[:, columns] - tile_x[group]

    for group in range(ny):
        @pl.when(jnp.logical_not(jnp.logical_and(holder, group == y)))
        def _():
            arrive(tile_y.at[group], r_ty.at[group])

        columns = pl.ds(nx * qx + group * qy, qy)
        out[:, columns] = rest[:, columns] - tile_y[group]

    for panel in (0, 1):
        arrive(solved.at[panel, :, 1 - core], r_out.at[panel])

    sent(diag.at[core], s_swap.at[0])
    sent(cross.at[core], s_swap.at[1])
    sent(loads.at[core], s_swap.at[2])
    for panel in (0, 1):
        sent(solved.at[panel, :, core], s_out.at[panel])
    for panel in (0, 1):
        sent(raw_x.at[core, panel], s_deal.at[panel, 0])
        sent(raw_y.at[core, panel], s_deal.at[panel, 1])

    for h in (0, 1):
        @pl.loop(0, rows)
        def _(step):
            peer = lax.rem(row + step, rows)

            @pl.when(jnp.logical_or(step > 0, jnp.logical_not(holder)))
            def _():
                sent(gathered.at[0, 0, 0], s_a.at[h, peer])

            @pl.when(jnp.logical_and(step > 0, holder))
            def _():
                sent(lower.at[0, 0], s_e.at[h, peer])

        @pl.loop(1, nz)
        def _(step):
            peer = lax.rem(z + step, nz)
            for sem in (s_b, s_c, s_f, s_g):
                sent(part_up.at[0, 0], sem.at[h, peer])

        @pl.loop(0, nz)
        def _(block):
            @pl.when(2 * block + core != row)
            def _():
                sent(part_cross.at[0, 0], s_d.at[h, block])

        for panel in (0, 1):
            for step in x_steps[panel:]:
                sent(along_x.at[0, 0, :, rows_of(0)], s_lx.at[h, panel, lax.rem(x + step, nx)])
            for step in y_steps[panel:]:
                sent(along_y.at[0, 0, :, rows_of(0)], s_ly.at[h, panel, lax.rem(y + step, ny)])

    @pl.loop(1, nx)
    def _(step):
        peer = lax.rem(x + step, nx)
        for panel in (0, 1):
            sent(raw_x.at[core, panel, 0], s_px.at[panel, peer])

    @pl.loop(1, ny)
    def _(step):
        peer = lax.rem(y + step, ny)
        for panel in (0, 1):
            sent(raw_y.at[core, panel, 0], s_py.at[panel, peer])

    @pl.loop(0, half)
    def _(offset):
        target = 2 * offset + core
        for owner in (0, 1):
            @pl.when(jnp.logical_not(jnp.logical_and(target == x, owner == core)))
            def _():
                sent(done_x.at[0, 0], s_tx.at[offset, owner])

    for axis in (0, 1):
        sent(own_block, s_far.at[axis])
        for step in z_steps:
            sent(own_block, s_fz.at[axis, lax.rem(z + step, nz)])

    for side in (0, 1):
        sent(relay_x.at[0], s_rx.at[side])
        for piece in (0, 1):
            sent(land_x.at[0, 0], s_sx.at[side, piece])

            @pl.when(jnp.logical_not(holder))
            def _():
                sent(land_y.at[0, first], s_sy.at[side, piece])

        @pl.when(holder)
        def _():
            sent(relay_y.at[0], s_ry.at[side])

    @pl.when(holder)
    def _():
        @pl.loop(0, ny)
        def _(peer):
            for owner in (0, 1):
                @pl.when(jnp.logical_not(jnp.logical_and(peer == y, owner == core)))
                def _():
                    sent(done_y.at[0, 0], s_ty.at[peer, owner])


def local(mesh, diag_inv, cross_block, coupling, panel_loads, rest_loads):
    rows, cols = mesh.shape["row"], mesh.shape["col"]
    nx = ny = math.isqrt(rows)
    nz, half = cols // 2, math.isqrt(rows) // 2
    _, height, width = panel_loads.shape
    span = rest_loads.shape[1]
    qx, qy = span // 2 // nx, span // 2 // ny
    f32, bf16 = jnp.float32, jnp.bfloat16
    vmem, dma = pltpu.VMEM, lambda *shape: pltpu.SemaphoreType.DMA(shape)
    block, piece = (height, width), (height // 2, width)
    whole = pl.BlockSpec(memory_space=pltpu.VMEM)
    solved, rest_updated = pl.pallas_call(
        functools.partial(solve_kernel, (rows, nx, ny, nz, height, width, qx, qy)),
        out_shape=(
            jax.ShapeDtypeStruct((2, nz, 2) + block, f32),
            jax.ShapeDtypeStruct((height, span), f32),
        ),
        in_specs=[pl.BlockSpec(memory_space=pltpu.HBM)] * 5,
        out_specs=(whole, whole),
        scratch_shapes=[
            vmem((2, 2, width, width), f32),
            vmem((2, width, width), f32),
            vmem((2,) + block, f32),
            vmem((height, span), f32),
            vmem((2, nz, 2) + piece, f32),
            vmem((2, nz) + piece, f32),
            vmem((2, nz) + piece, f32),
            vmem((2, nz, height // 2, 2 * width), f32),
            vmem((2, rows, height // 2, 2 * width), f32),
            vmem((2, nz, height // 2, 2 * width), f32),
            vmem((2, nz) + piece, f32),
            vmem((2, nz) + piece, f32),
            vmem((2, 2, nx, width, qx), f32),
            vmem((2, 2, ny, width, qy), f32),
            vmem((2, 2 * nx * width, qx), bf16),
            vmem((2, 2 * nx * width, qx), bf16),
            vmem((2, 2 * ny * width, qy), bf16),
            vmem((2, 2 * ny * width, qy), bf16),
            vmem((2, nx, nz) + block, f32),
            vmem((2, ny, nz) + block, f32),
            vmem((ny, half, 2, height, qx), f32),
            vmem((2, half, 2, height, qx), f32),
            vmem((2, 2, height, qx), f32),
            vmem((half, ny, 2, height, qy), f32),
            vmem((2, ny, 2, height, qy), f32),
            vmem((2, half, 2, height, qy), f32),
            vmem((half, 2, height, qx), f32),
            vmem((ny, 2, height, qy), f32),
            vmem((nx, height, qx), f32),
            vmem((ny, height, qy), f32),
            dma(8), dma(3), dma(3),
            dma(2, rows), dma(2, nz, 2),
            dma(2, nz), dma(2, nz), dma(2, nz), dma(2, nz),
            dma(2, nz), dma(2, rows), dma(2, rows), dma(2, nz),
            dma(2, nz), dma(2, nz), dma(2, nz), dma(2, nz),
            dma(2, nx), dma(2, nx), dma(2, ny), dma(2, ny), dma(2, 2), dma(2, 2),
            dma(2, 2, nx), dma(2, 2, nx), dma(2, 2, ny), dma(2, 2, ny),
            dma(2, 2), dma(2, 2), dma(2, 2), dma(2, 2), dma(2), dma(2), dma(2), dma(2),
            dma(2), dma(2), dma(2, nz), dma(2, nz),
            dma(half, 2), dma(nx), dma(ny, 2), dma(ny),
            dma(2), dma(2),
        ],
        compiler_params=pltpu.CompilerParams(
            collective_id=0, has_side_effects=True, vmem_limit_bytes=42 * 2**20
        ),
    )(*(pltpu.with_memory_space_constraint(arg, pltpu.HBM) for arg in (diag_inv, cross_block, coupling, panel_loads, rest_loads)))
    return solved.reshape(2, rows * height, width), rest_updated


def solution(mesh):
    in_specs = (
        P(None, "col", "row"),
        P("row", "col"),
        P(None, "row", "col"),
        P(None, "row", "col"),
        P("row", "col"),
    )
    out_specs = (P(None, None, "row"), P("row", "col"))
    return jax.shard_map(
        functools.partial(local, mesh), mesh=mesh, in_specs=in_specs, out_specs=out_specs, check_vma=False
    )
```

```python
import functools
import math

import jax
import jax.numpy as jnp
from jax import lax
from jax.experimental import pallas as pl
from jax.experimental.pallas import tpu as pltpu
from jax.sharding import PartitionSpec as P

MESH = pl.DeviceIdType.MESH


def halves(value):
    high = value.astype(jnp.bfloat16)
    low = (value - high.astype(jnp.float32)).astype(jnp.bfloat16)
    return high, low


def product(left_halves, right_halves):
    left_high, left_low = left_halves
    right_high, right_low = right_halves
    dot = functools.partial(jnp.dot, preferred_element_type=jnp.float32)
    rows = left_high.shape[0]
    both = dot(jnp.concatenate([left_high, left_low], axis=0), right_high)
    return both[:rows] + (both[rows:] + dot(left_high, right_low))


def farthest_first(size):
    return sorted(range(1, size), key=lambda step: -min(step, size - step))


def solve_kernel(
    dims,
    diag_hbm, cross_hbm, coupling_hbm, loads_hbm, rest_hbm,
    solved, out,
    diag, cross, loads, rest,
    gathered, part_up, land_up, part_cross, land_cross, lower, part_low, land_low,
    raw_x, raw_y, high_x, low_x, high_y, low_y,
    along_x, along_y, sum_x, land_x, relay_x, sum_y, land_y, relay_y, done_x, done_y, tile_x, tile_y,
    local_sem, s_swap, r_swap, s_a, r_a, s_b, r_b, s_c, r_c, s_d, r_d, s_e, r_e, s_f, r_f, s_g, r_g,
    s_px, r_px, s_py, r_py, s_deal, r_deal, s_lx, r_lx, s_ly, r_ly,
    s_sx, r_sx, s_sy, r_sy, s_rx, r_rx, s_ry, r_ry, s_far, r_far, s_fz, r_fz, s_tx, r_tx, s_ty, r_ty, s_out, r_out,
):
    rows, nx, ny, nz, height, width, qx, qy = dims
    half, part = nx // 2, height // 2
    x_steps, y_steps, z_steps = farthest_first(nx), farthest_first(ny), farthest_first(nz)
    plane_steps = sorted(
        ((dy, dx) for dy in range(ny) for dx in range(nx) if (dy, dx) != (0, 0)),
        key=lambda step: -min(step[0], ny - step[0]) - min(step[1], nx - step[1]),
    )
    row, col = lax.axis_index("row"), lax.axis_index("col")
    y, x = lax.div(row, nx), lax.rem(row, nx)
    z, core = lax.div(col, 2), lax.rem(col, 2)
    parity, slot = lax.rem(row, 2), lax.div(row, 2)
    holder = parity == core
    sibling = 2 * z + 1 - core

    def beside(step):
        return lax.rem(y + step[0], ny) * nx + lax.rem(x + step[1], nx)

    def send(source, target, send_sem, recv_sem, to_row, to_col):
        copy = pltpu.make_async_remote_copy(
            src_ref=source, dst_ref=target, send_sem=send_sem, recv_sem=recv_sem,
            device_id={"row": to_row, "col": to_col}, device_id_type=MESH,
        )
        copy.start()

    def arrive(place, recv_sem):
        pltpu.make_async_remote_copy(
            src_ref=place, dst_ref=place, send_sem=s_swap.at[0], recv_sem=recv_sem,
            device_id={"row": row, "col": sibling}, device_id_type=MESH,
        ).wait_recv()

    def sent(place, send_sem):
        pltpu.make_async_remote_copy(
            src_ref=place, dst_ref=place, send_sem=send_sem, recv_sem=r_swap.at[0],
            device_id={"row": row, "col": sibling}, device_id_type=MESH,
        ).wait_send()

    own_copies = [
        pltpu.make_async_copy(diag_hbm, diag.at[core], local_sem.at[0]),
        pltpu.make_async_copy(cross_hbm, cross.at[core], local_sem.at[1]),
        pltpu.make_async_copy(loads_hbm.at[0], loads.at[core], local_sem.at[2]),
        pltpu.make_async_copy(rest_hbm, rest, local_sem.at[3]),
        pltpu.make_async_copy(
            coupling_hbm.at[:, :, pl.ds(pl.multiple_of(x * qx, qx), qx)], raw_x.at[core, :, x], local_sem.at[4]
        ),
        pltpu.make_async_copy(
            coupling_hbm.at[:, :, pl.ds(pl.multiple_of(nx * qx + y * qy, qy), qy)], raw_y.at[core, :, y], local_sem.at[5]
        ),
    ]
    for copy in own_copies:
        copy.start()
    own_upper = [
        pltpu.make_async_copy(loads_hbm.at[1, pl.ds(h * part, part)], gathered.at[h, slot, core], local_sem.at[6 + h])
        for h in (0, 1)
    ]

    @pl.when(holder)
    def _():
        for copy in own_upper:
            copy.start()

    barrier = pltpu.get_barrier_semaphore()

    @pl.loop(0, rows)
    def _(step):
        peer = lax.rem(row + step, rows)
        pl.semaphore_signal(barrier, inc=1, device_id={"row": peer, "col": sibling}, device_id_type=MESH)

        @pl.when(step > 0)
        def _():
            pl.semaphore_signal(barrier, inc=1, device_id={"row": peer, "col": col}, device_id_type=MESH)

    @pl.loop(1, nz)
    def _(step):
        peer = lax.rem(z + step, nz)
        pl.semaphore_signal(barrier, inc=1, device_id={"row": row, "col": 2 * peer + core}, device_id_type=MESH)

    pl.semaphore_wait(barrier, 2 * rows - 1 + nz - 1)

    def rows_of(h):
        return pl.ds(h * part, part)

    def scatter_z(h, parts, landing, s_sem, r_sem):
        for step in z_steps:
            peer = lax.rem(z + step, nz)
            send(parts.at[h, peer], landing.at[h, z], s_sem.at[h, peer], r_sem.at[h, z], row, 2 * peer + core)

    def total_z(h, parts, landing, r_sem):
        value = parts[h, z]
        for step in z_steps:
            peer = lax.rem(z + step, nz)
            arrive(landing.at[h, peer], r_sem.at[h, peer])
            value = value + landing[h, peer]
        return value

    def spread_z(h, panel, value, s_sem, r_sem):
        place = solved.at[panel, z, core, rows_of(h)]
        place[...] = value
        for step in z_steps:
            peer = lax.rem(z + step, nz)
            send(place, place, s_sem.at[h, peer], r_sem.at[h, z], row, 2 * peer + core)

    def found_z(h, panel, r_sem):
        for step in z_steps:
            peer = lax.rem(z + step, nz)
            arrive(solved.at[panel, peer, core, rows_of(h)], r_sem.at[h, peer])
        found = solved[panel, :, core, rows_of(h)]
        along_x[panel, x, :, rows_of(h)] = found
        along_y[panel, y, :, rows_of(h)] = found
        return found.reshape(nz * part, width)

    def gather_upper(h):
        source = loads_hbm.at[1, rows_of(h)]
        target = gathered.at[h, slot, core]
        for step in plane_steps:
            peer = beside(step)
            send(source, target, s_a.at[h, peer], r_a.at[h, slot, core], peer, 2 * z + parity)

        @pl.when(jnp.logical_not(holder))
        def _():
            send(source, target, s_a.at[h, row], r_a.at[h, slot, core], row, sibling)

    def multiply_upper(h):
        for block in range(nz):
            for source in (0, 1):
                @pl.when(jnp.logical_not(jnp.logical_and(2 * block + core == row, source == core)))
                def _():
                    arrive(gathered.at[h, block, source], r_a.at[h, block, source])
        left = jnp.concatenate([gathered[h, :, source].reshape(nz * part, width) for source in (0, 1)], axis=1)
        part_up[h] = product(halves(left), upper_diag).reshape(nz, part, width)
        scatter_z(h, part_up, land_up, s_b, r_b)

    def multiply_cross(h):
        upper = found_z(h, 1, r_c)
        part_cross[h] = product(halves(upper), cross_halves).reshape(nz, part, 2 * width)
        for step in range(nz):
            block = lax.rem(slot + nz // 2 + step, nz)
            owner = 2 * block + core

            @pl.when(owner != row)
            def _():
                send(part_cross.at[h, block], land_cross.at[h, row], s_d.at[h, block], r_d.at[h, row], owner, col)

    def reduce_cross(h):
        @pl.when(holder)
        def _():
            value = jnp.concatenate([loads[0, rows_of(h)], loads[1, rows_of(h)]], axis=1) - part_cross[h, slot]
            for step in plane_steps:
                peer = beside(step)
                arrive(land_cross.at[h, peer], r_d.at[h, peer])
                value = value - land_cross[h, peer]
            place = lower.at[h, slot]
            place[...] = value
            for step in plane_steps:
                peer = beside(step)
                send(place, place, s_e.at[h, peer], r_e.at[h, slot], peer, col)

    def multiply_lower(h):
        for block in range(nz):
            @pl.when(2 * block + core != row)
            def _():
                arrive(lower.at[h, block], r_e.at[h, block])
        part_low[h] = product(halves(lower[h].reshape(nz * part, 2 * width)), lower_diag).reshape(nz, part, width)
        scatter_z(h, part_low, land_low, s_f, r_f)

    def forward(h, panel):
        for step in x_steps[panel:]:
            peer = lax.rem(x + step, nx)
            place = along_x.at[panel, x, :, rows_of(h)]
            send(place, place, s_lx.at[h, panel, peer], r_lx.at[h, panel, x], y * nx + peer, col)
        for step in y_steps[panel:]:
            peer = lax.rem(y + step, ny)
            place = along_y.at[panel, y, :, rows_of(h)]
            send(place, place, s_ly.at[h, panel, peer], r_ly.at[h, panel, y], peer * nx + x, col)

    def deal(panel):
        for step in x_steps:
            peer = lax.rem(x + step, nx)
            send(
                coupling_hbm.at[panel, :, pl.ds(pl.multiple_of(peer * qx, qx), qx)], raw_x.at[core, panel, x],
                s_px.at[panel, peer], r_px.at[panel, x], y * nx + peer, col,
            )
        for step in y_steps:
            peer = lax.rem(y + step, ny)
            send(
                coupling_hbm.at[panel, :, pl.ds(pl.multiple_of(nx * qx + peer * qy, qy), qy)], raw_y.at[core, panel, y],
                s_py.at[panel, peer], r_py.at[panel, y], peer * nx + x, col,
            )

    def share_dealt(panel):
        for step in x_steps:
            peer = lax.rem(x + step, nx)
            arrive(raw_x.at[core, panel, peer], r_px.at[panel, peer])
        send(raw_x.at[core, panel], raw_x.at[core, panel], s_deal.at[panel, 0], r_deal.at[panel, 0], row, sibling)
        for step in y_steps:
            peer = lax.rem(y + step, ny)
            arrive(raw_y.at[core, panel, peer], r_py.at[panel, peer])
        send(raw_y.at[core, panel], raw_y.at[core, panel], s_deal.at[panel, 1], r_deal.at[panel, 1], row, sibling)

    def split_dealt(panel):
        arrive(raw_x.at[1 - core, panel], r_deal.at[panel, 0])
        arrive(raw_y.at[1 - core, panel], r_deal.at[panel, 1])
        for raw, high, low, groups in ((raw_x, high_x, low_x, nx), (raw_y, high_y, low_y, ny)):
            @pl.loop(0, 2 * groups)
            def _(index):
                owner, group = lax.div(index, groups), lax.rem(index, groups)
                start = pl.multiple_of((panel * groups + group) * width, width)
                block_high, block_low = halves(raw[owner, panel, group])
                high[owner, pl.ds(start, width)] = block_high
                low[owner, pl.ds(start, width)] = block_low

    send(diag_hbm, diag.at[core], s_swap.at[0], r_swap.at[0], row, sibling)
    gather_upper(0)
    gather_upper(1)
    send(cross_hbm, cross.at[core], s_swap.at[1], r_swap.at[1], row, sibling)
    send(loads_hbm.at[0], loads.at[core], s_swap.at[2], r_swap.at[2], row, sibling)

    own_copies[0].wait()
    arrive(diag.at[1 - core], r_swap.at[0])

    @pl.when(holder)
    def _():
        for copy in own_upper:
            copy.wait()

    upper_diag = halves(diag[:, 1].reshape(2 * width, width))
    multiply_upper(0)
    deal(1)
    multiply_upper(1)

    own_copies[1].wait()
    arrive(cross.at[1 - core], r_swap.at[1])
    cross_halves = halves(jnp.concatenate([cross[0], cross[1]], axis=1))
    for h in (0, 1):
        spread_z(h, 1, total_z(h, part_up, land_up, r_b), s_c, r_c)

    x_far, y_far = lax.rem(x + half, nx), lax.rem(y + half, ny)
    own_block = solved.at[1, z, core]
    send(own_block, along_x.at[1, x, z], s_far.at[0], r_far.at[0], y * nx + x_far, col)
    send(own_block, along_y.at[1, y, z], s_far.at[1], r_far.at[1], y_far * nx + x, col)

    own_copies[2].wait()
    arrive(loads.at[1 - core], r_swap.at[2])
    for h in (0, 1):
        multiply_cross(h)
    far_places = (along_x.at[1, x_far], along_y.at[1, y_far])
    for axis in (0, 1):
        place = far_places[axis].at[z]
        arrive(place, r_far.at[axis])
        for step in z_steps:
            peer = lax.rem(z + step, nz)
            send(place, place, s_fz.at[axis, peer], r_fz.at[axis, z], row, 2 * peer + core)
    for h in (0, 1):
        reduce_cross(h)
    deal(0)

    lower_diag = halves(diag[:, 0].reshape(2 * width, width))
    for h in (0, 1):
        multiply_lower(h)

    for h in (0, 1):
        forward(h, 1)
    send(solved.at[1, :, core], solved.at[1, :, core], s_out.at[1], r_out.at[1], row, sibling)

    own_copies[4].wait()
    own_copies[5].wait()
    for h in (0, 1):
        spread_z(h, 0, total_z(h, part_low, land_low, r_f), s_g, r_g)
    share_dealt(1)
    share_dealt(0)
    for h in (0, 1):
        found_z(h, 0, r_g)
        forward(h, 0)
    send(solved.at[0, :, core], solved.at[0, :, core], s_out.at[0], r_out.at[0], row, sibling)
    split_dealt(1)
    split_dealt(0)

    for h in (0, 1):
        for panel in (1, 0):
            for step in x_steps[panel:]:
                peer = lax.rem(x + step, nx)
                arrive(along_x.at[panel, peer, :, rows_of(h)], r_lx.at[h, panel, peer])
            for step in y_steps[panel:]:
                peer = lax.rem(y + step, ny)
                arrive(along_y.at[panel, peer, :, rows_of(h)], r_ly.at[h, panel, peer])

    for axis in (0, 1):
        for step in z_steps:
            peer = lax.rem(z + step, nz)
            arrive(far_places[axis].at[peer], r_fz.at[axis, peer])

    y_up, y_down = lax.rem(y + 1, ny), lax.rem(y + ny - 1, ny)
    x_up, x_down = lax.rem(x + 1, nx), lax.rem(x + nx - 1, nx)
    row_up, row_down = y_up * nx + x, y_down * nx + x
    side_up, side_down = y * nx + x_up, y * nx + x_down
    own_offset = lax.div(x, 2)
    up_offset, down_offset = lax.div(x_up, 2), lax.div(x_down, 2)
    first, last = pl.ds(0, half), pl.ds(half, half)
    bridge = jnp.logical_not(holder)

    def tile_over_y(peer, owner):
        left = halves(jnp.concatenate(
            [
                along_x[panel, group, pl.ds(peer * half, half)].reshape(half * height, width)
                for panel in (0, 1) for group in range(nx)
            ],
            axis=1,
        ))
        value = product(left, (high_x[owner], low_x[owner]))
        sum_x[peer, :, owner] = value.reshape(half, height, qx)

    def tile_over_x(offset, start, owner):
        left = halves(jnp.concatenate(
            [
                jnp.concatenate([along_y[panel, group, (start + part) * half + offset] for part in range(half)], axis=0)
                for panel in (0, 1) for group in range(ny)
            ],
            axis=1,
        ))
        value = product(left, (high_y[owner], low_y[owner]))
        sum_y[offset, pl.ds(start, half), owner] = value.reshape(half, height, qy)

    def early(owner):
        tile_over_x(jnp.where(holder, 1 - own_offset, up_offset), jnp.where(holder, 0, half), owner)

        @pl.when(holder)
        def _():
            send(sum_y.at[1 - own_offset, first, owner], relay_y.at[0, :, owner],
                 s_ry.at[owner, 0], r_ry.at[owner, 0], side_up, col)

        @pl.when(bridge)
        def _():
            send(sum_y.at[up_offset, last, owner], land_y.at[0, last, owner],
                 s_sy.at[owner, 0, 1], r_sy.at[owner, 0, 1], side_up, col)

        tile_over_y(y_far, owner)
        send(sum_x.at[y_far, 0, owner], relay_x.at[0, owner], s_rx.at[owner, 0], r_rx.at[owner, 0], row_up, col)
        send(sum_x.at[y_far, 1, owner], relay_x.at[1, owner], s_rx.at[owner, 1], r_rx.at[owner, 1], row_down, col)

        tile_over_x(jnp.where(holder, 1 - own_offset, down_offset), jnp.where(holder, half, 0), owner)

        @pl.when(holder)
        def _():
            send(sum_y.at[1 - own_offset, last, owner], relay_y.at[1, :, owner],
                 s_ry.at[owner, 1], r_ry.at[owner, 1], side_down, col)

        @pl.when(bridge)
        def _():
            send(sum_y.at[down_offset, first, owner], land_y.at[1, first, owner],
                 s_sy.at[owner, 1, 0], r_sy.at[owner, 1, 0], side_down, col)

        tile_over_y(y_up, owner)
        send(sum_x.at[y_up, 1, owner], land_x.at[0, 1, owner], s_sx.at[owner, 0, 1], r_sx.at[owner, 0, 1], row_up, col)
        tile_over_y(y_down, owner)
        send(sum_x.at[y_down, 0, owner], land_x.at[1, 0, owner], s_sx.at[owner, 1, 0], r_sx.at[owner, 1, 0], row_down, col)

    def late(owner):
        tile_over_x(jnp.where(holder, own_offset, up_offset), 0, owner)

        @pl.when(bridge)
        def _():
            arrive(relay_y.at[0, :, owner], r_ry.at[owner, 0])
            sum_y[up_offset, first, owner] = sum_y[up_offset, first, owner] + relay_y[0, :, owner]
            send(sum_y.at[up_offset, first, owner], land_y.at[0, first, owner],
                 s_sy.at[owner, 0, 0], r_sy.at[owner, 0, 0], side_up, col)

        arrive(relay_x.at[0, owner], r_rx.at[owner, 0])
        sum_x[y_up, 0, owner] = sum_x[y_up, 0, owner] + relay_x[0, owner]
        send(sum_x.at[y_up, 0, owner], land_x.at[0, 0, owner], s_sx.at[owner, 0, 0], r_sx.at[owner, 0, 0], row_up, col)
        arrive(relay_x.at[1, owner], r_rx.at[owner, 1])
        sum_x[y_down, 1, owner] = sum_x[y_down, 1, owner] + relay_x[1, owner]
        send(sum_x.at[y_down, 1, owner], land_x.at[1, 1, owner], s_sx.at[owner, 1, 1], r_sx.at[owner, 1, 1], row_down, col)

        tile_over_x(jnp.where(holder, own_offset, down_offset), half, owner)

        @pl.when(bridge)
        def _():
            arrive(relay_y.at[1, :, owner], r_ry.at[owner, 1])
            sum_y[down_offset, last, owner] = sum_y[down_offset, last, owner] + relay_y[1, :, owner]
            send(sum_y.at[down_offset, last, owner], land_y.at[1, last, owner],
                 s_sy.at[owner, 1, 1], r_sy.at[owner, 1, 1], side_down, col)

        tile_over_y(y, owner)

    def finish(owner):
        for offset in range(half):
            for side in (0, 1):
                arrive(land_x.at[side, offset, owner], r_sx.at[owner, side, offset])
            done_x[offset, owner] = sum_x[y, offset, owner] + land_x[0, offset, owner] + land_x[1, offset, owner]
            target = 2 * offset + core

            @pl.when(jnp.logical_not(jnp.logical_and(target == x, owner == core)))
            def _():
                send(
                    done_x.at[offset, owner], tile_x.at[x], s_tx.at[offset, owner], r_tx.at[x],
                    y * nx + target, 2 * z + owner,
                )

        @pl.when(holder)
        def _():
            for peer in range(ny):
                if peer % half == 0:
                    for side in (0, 1):
                        arrive(land_y.at[side, pl.ds(peer, half), owner], r_sy.at[owner, side, peer // half])
                done_y[peer, owner] = sum_y[own_offset, peer, owner] + land_y[0, peer, owner] + land_y[1, peer, owner]

                @pl.when(jnp.logical_not(jnp.logical_and(peer == y, owner == core)))
                def _():
                    send(
                        done_y.at[peer, owner], tile_y.at[y], s_ty.at[peer, owner], r_ty.at[y],
                        peer * nx + x, 2 * z + owner,
                    )

    early(0)
    late(0)
    early(1)
    finish(0)
    late(1)
    finish(1)
    own_copies[3].wait()

    @pl.when(holder)
    def _():
        tile_x[x] = done_x[own_offset, core]
        tile_y[y] = done_y[y, core]

    for group in range(nx):
        @pl.when(jnp.logical_not(jnp.logical_and(holder, group == x)))
        def _():
            arrive(tile_x.at[group], r_tx.at[group])

        columns = pl.ds(group * qx, qx)
        out[:, columns] = rest[:, columns] - tile_x[group]

    for group in range(ny):
        @pl.when(jnp.logical_not(jnp.logical_and(holder, group == y)))
        def _():
            arrive(tile_y.at[group], r_ty.at[group])

        columns = pl.ds(nx * qx + group * qy, qy)
        out[:, columns] = rest[:, columns] - tile_y[group]

    for panel in (0, 1):
        arrive(solved.at[panel, :, 1 - core], r_out.at[panel])

    sent(diag.at[core], s_swap.at[0])
    sent(cross.at[core], s_swap.at[1])
    sent(loads.at[core], s_swap.at[2])
    for panel in (0, 1):
        sent(solved.at[panel, :, core], s_out.at[panel])
    for panel in (0, 1):
        sent(raw_x.at[core, panel], s_deal.at[panel, 0])
        sent(raw_y.at[core, panel], s_deal.at[panel, 1])

    for h in (0, 1):
        @pl.loop(0, rows)
        def _(step):
            peer = lax.rem(row + step, rows)

            @pl.when(jnp.logical_or(step > 0, jnp.logical_not(holder)))
            def _():
                sent(gathered.at[0, 0, 0], s_a.at[h, peer])

            @pl.when(jnp.logical_and(step > 0, holder))
            def _():
                sent(lower.at[0, 0], s_e.at[h, peer])

        @pl.loop(1, nz)
        def _(step):
            peer = lax.rem(z + step, nz)
            for sem in (s_b, s_c, s_f, s_g):
                sent(part_up.at[0, 0], sem.at[h, peer])

        @pl.loop(0, nz)
        def _(block):
            @pl.when(2 * block + core != row)
            def _():
                sent(part_cross.at[0, 0], s_d.at[h, block])

        for panel in (0, 1):
            for step in x_steps[panel:]:
                sent(along_x.at[0, 0, :, rows_of(0)], s_lx.at[h, panel, lax.rem(x + step, nx)])
            for step in y_steps[panel:]:
                sent(along_y.at[0, 0, :, rows_of(0)], s_ly.at[h, panel, lax.rem(y + step, ny)])

    @pl.loop(1, nx)
    def _(step):
        peer = lax.rem(x + step, nx)
        for panel in (0, 1):
            sent(raw_x.at[core, panel, 0], s_px.at[panel, peer])

    @pl.loop(1, ny)
    def _(step):
        peer = lax.rem(y + step, ny)
        for panel in (0, 1):
            sent(raw_y.at[core, panel, 0], s_py.at[panel, peer])

    @pl.loop(0, half)
    def _(offset):
        target = 2 * offset + core
        for owner in (0, 1):
            @pl.when(jnp.logical_not(jnp.logical_and(target == x, owner == core)))
            def _():
                sent(done_x.at[0, 0], s_tx.at[offset, owner])

    for axis in (0, 1):
        sent(own_block, s_far.at[axis])
        for step in z_steps:
            sent(own_block, s_fz.at[axis, lax.rem(z + step, nz)])

    for owner in (0, 1):
        for side in (0, 1):
            sent(relay_x.at[0, 0], s_rx.at[owner, side])
            for piece in (0, 1):
                sent(land_x.at[0, 0, 0], s_sx.at[owner, side, piece])

                @pl.when(bridge)
                def _():
                    sent(land_y.at[0, first, 0], s_sy.at[owner, side, piece])

            @pl.when(holder)
            def _():
                sent(relay_y.at[0, :, 0], s_ry.at[owner, side])

    @pl.when(holder)
    def _():
        @pl.loop(0, ny)
        def _(peer):
            for owner in (0, 1):
                @pl.when(jnp.logical_not(jnp.logical_and(peer == y, owner == core)))
                def _():
                    sent(done_y.at[0, 0], s_ty.at[peer, owner])


def local(mesh, diag_inv, cross_block, coupling, panel_loads, rest_loads):
    rows, cols = mesh.shape["row"], mesh.shape["col"]
    nx = ny = math.isqrt(rows)
    nz, half = cols // 2, math.isqrt(rows) // 2
    _, height, width = panel_loads.shape
    span = rest_loads.shape[1]
    qx, qy = span // 2 // nx, span // 2 // ny
    f32, bf16 = jnp.float32, jnp.bfloat16
    vmem, dma = pltpu.VMEM, lambda *shape: pltpu.SemaphoreType.DMA(shape)
    block, piece = (height, width), (height // 2, width)
    whole = pl.BlockSpec(memory_space=pltpu.VMEM)
    solved, rest_updated = pl.pallas_call(
        functools.partial(solve_kernel, (rows, nx, ny, nz, height, width, qx, qy)),
        out_shape=(
            jax.ShapeDtypeStruct((2, nz, 2) + block, f32),
            jax.ShapeDtypeStruct((height, span), f32),
        ),
        in_specs=[pl.BlockSpec(memory_space=pltpu.HBM)] * 5,
        out_specs=(whole, whole),
        scratch_shapes=[
            vmem((2, 2, width, width), f32),
            vmem((2, width, width), f32),
            vmem((2,) + block, f32),
            vmem((height, span), f32),
            vmem((2, nz, 2) + piece, f32),
            vmem((2, nz) + piece, f32),
            vmem((2, nz) + piece, f32),
            vmem((2, nz, height // 2, 2 * width), f32),
            vmem((2, rows, height // 2, 2 * width), f32),
            vmem((2, nz, height // 2, 2 * width), f32),
            vmem((2, nz) + piece, f32),
            vmem((2, nz) + piece, f32),
            vmem((2, 2, nx, width, qx), f32),
            vmem((2, 2, ny, width, qy), f32),
            vmem((2, 2 * nx * width, qx), bf16),
            vmem((2, 2 * nx * width, qx), bf16),
            vmem((2, 2 * ny * width, qy), bf16),
            vmem((2, 2 * ny * width, qy), bf16),
            vmem((2, nx, nz) + block, f32),
            vmem((2, ny, nz) + block, f32),
            vmem((ny, half, 2, height, qx), f32),
            vmem((2, half, 2, height, qx), f32),
            vmem((2, 2, height, qx), f32),
            vmem((half, ny, 2, height, qy), f32),
            vmem((2, ny, 2, height, qy), f32),
            vmem((2, half, 2, height, qy), f32),
            vmem((half, 2, height, qx), f32),
            vmem((ny, 2, height, qy), f32),
            vmem((nx, height, qx), f32),
            vmem((ny, height, qy), f32),
            dma(8), dma(3), dma(3),
            dma(2, rows), dma(2, nz, 2),
            dma(2, nz), dma(2, nz), dma(2, nz), dma(2, nz),
            dma(2, nz), dma(2, rows), dma(2, rows), dma(2, nz),
            dma(2, nz), dma(2, nz), dma(2, nz), dma(2, nz),
            dma(2, nx), dma(2, nx), dma(2, ny), dma(2, ny), dma(2, 2), dma(2, 2),
            dma(2, 2, nx), dma(2, 2, nx), dma(2, 2, ny), dma(2, 2, ny),
            dma(2, 2, 2), dma(2, 2, 2), dma(2, 2, 2), dma(2, 2, 2), dma(2, 2), dma(2, 2), dma(2, 2), dma(2, 2),
            dma(2), dma(2), dma(2, nz), dma(2, nz),
            dma(half, 2), dma(nx), dma(ny, 2), dma(ny),
            dma(2), dma(2),
        ],
        compiler_params=pltpu.CompilerParams(
            collective_id=0, has_side_effects=True, vmem_limit_bytes=42 * 2**20
        ),
    )(*(pltpu.with_memory_space_constraint(arg, pltpu.HBM) for arg in (diag_inv, cross_block, coupling, panel_loads, rest_loads)))
    return solved.reshape(2, rows * height, width), rest_updated


def solution(mesh):
    in_specs = (
        P(None, "col", "row"),
        P("row", "col"),
        P(None, "row", "col"),
        P(None, "row", "col"),
        P("row", "col"),
    )
    out_specs = (P(None, None, "row"), P("row", "col"))
    return jax.shard_map(
        functools.partial(local, mesh), mesh=mesh, in_specs=in_specs, out_specs=out_specs, check_vma=False
    )
```

```python
import functools
import math

import jax
import jax.numpy as jnp
from jax import lax
from jax.experimental import pallas as pl
from jax.experimental.pallas import tpu as pltpu
from jax.sharding import PartitionSpec as P

MESH = pl.DeviceIdType.MESH


def halves(value):
    high = value.astype(jnp.bfloat16)
    low = (value - high.astype(jnp.float32)).astype(jnp.bfloat16)
    return high, low


def product(left_halves, right_halves):
    left_high, left_low = left_halves
    right_high, right_low = right_halves
    dot = functools.partial(jnp.dot, preferred_element_type=jnp.float32)
    rows = left_high.shape[0]
    both = dot(jnp.concatenate([left_high, left_low], axis=0), right_high)
    return both[:rows] + (both[rows:] + dot(left_high, right_low))


def farthest_first(size):
    return sorted(range(1, size), key=lambda step: -min(step, size - step))


def solve_kernel(
    dims,
    diag_hbm, cross_hbm, coupling_hbm, loads_hbm, rest_hbm,
    solved, out,
    diag, cross, loads, rest,
    gathered, part_up, land_up, part_cross, land_cross, lower, part_low, land_low,
    raw_x, raw_y, high_x, low_x, high_y, low_y,
    along_x, along_y, sum_x, land_x, relay_x, sum_y, land_y, relay_y, done_x, done_y, tile_x, tile_y,
    local_sem, s_swap, r_swap, s_a, r_a, s_b, r_b, s_c, r_c, s_d, r_d, s_e, r_e, s_f, r_f, s_g, r_g,
    s_px, r_px, s_py, r_py, s_deal, r_deal, s_lx, r_lx, s_ly, r_ly,
    s_sx, r_sx, s_sy, r_sy, s_rx, r_rx, s_ry, r_ry, s_far, r_far, s_fz, r_fz, s_tx, r_tx, s_ty, r_ty, s_out, r_out,
):
    rows, nx, ny, nz, height, width, qx, qy = dims
    half, part = nx // 2, height // 2
    x_steps, y_steps, z_steps = farthest_first(nx), farthest_first(ny), farthest_first(nz)
    plane_steps = sorted(
        ((dy, dx) for dy in range(ny) for dx in range(nx) if (dy, dx) != (0, 0)),
        key=lambda step: -min(step[0], ny - step[0]) - min(step[1], nx - step[1]),
    )
    row, col = lax.axis_index("row"), lax.axis_index("col")
    y, x = lax.div(row, nx), lax.rem(row, nx)
    z, core = lax.div(col, 2), lax.rem(col, 2)
    parity, slot = lax.rem(row, 2), lax.div(row, 2)
    holder = parity == core
    sibling = 2 * z + 1 - core

    def beside(step):
        return lax.rem(y + step[0], ny) * nx + lax.rem(x + step[1], nx)

    def send(source, target, send_sem, recv_sem, to_row, to_col):
        copy = pltpu.make_async_remote_copy(
            src_ref=source, dst_ref=target, send_sem=send_sem, recv_sem=recv_sem,
            device_id={"row": to_row, "col": to_col}, device_id_type=MESH,
        )
        copy.start()

    def arrive(place, recv_sem):
        pltpu.make_async_remote_copy(
            src_ref=place, dst_ref=place, send_sem=s_swap.at[0], recv_sem=recv_sem,
            device_id={"row": row, "col": sibling}, device_id_type=MESH,
        ).wait_recv()

    def sent(place, send_sem):
        pltpu.make_async_remote_copy(
            src_ref=place, dst_ref=place, send_sem=send_sem, recv_sem=r_swap.at[0],
            device_id={"row": row, "col": sibling}, device_id_type=MESH,
        ).wait_send()

    own_copies = [
        pltpu.make_async_copy(diag_hbm, diag.at[core], local_sem.at[0]),
        pltpu.make_async_copy(cross_hbm, cross.at[core], local_sem.at[1]),
        pltpu.make_async_copy(loads_hbm.at[0], loads.at[core], local_sem.at[2]),
        pltpu.make_async_copy(rest_hbm, rest, local_sem.at[3]),
        pltpu.make_async_copy(
            coupling_hbm.at[:, :, pl.ds(pl.multiple_of(x * qx, qx), qx)], raw_x.at[core, :, x], local_sem.at[4]
        ),
        pltpu.make_async_copy(
            coupling_hbm.at[:, :, pl.ds(pl.multiple_of(nx * qx + y * qy, qy), qy)], raw_y.at[core, :, y], local_sem.at[5]
        ),
    ]
    for copy in own_copies:
        copy.start()
    own_upper = [
        pltpu.make_async_copy(loads_hbm.at[1, pl.ds(h * part, part)], gathered.at[h, slot, core], local_sem.at[6 + h])
        for h in (0, 1)
    ]

    @pl.when(holder)
    def _():
        for copy in own_upper:
            copy.start()

    barrier = pltpu.get_barrier_semaphore()

    def greet(to_row, to_col):
        pl.semaphore_signal(barrier, inc=1, device_id={"row": to_row, "col": to_col}, device_id_type=MESH)

    for step in z_steps:
        greet(row, 2 * lax.rem(z + step, nz) + core)
    for step in plane_steps:
        greet(beside(step), col)
        greet(beside(step), sibling)
    greet(row, sibling)

    pl.semaphore_wait(barrier, 2 * rows - 1 + nz - 1)

    def rows_of(h):
        return pl.ds(h * part, part)

    def scatter_z(h, parts, landing, s_sem, r_sem):
        for step in z_steps:
            peer = lax.rem(z + step, nz)
            send(parts.at[h, peer], landing.at[h, z], s_sem.at[h, peer], r_sem.at[h, z], row, 2 * peer + core)

    def total_z(h, parts, landing, r_sem):
        value = parts[h, z]
        for step in z_steps:
            peer = lax.rem(z + step, nz)
            arrive(landing.at[h, peer], r_sem.at[h, peer])
            value = value + landing[h, peer]
        return value

    def spread_z(h, panel, value, s_sem, r_sem):
        place = solved.at[panel, z, core, rows_of(h)]
        place[...] = value
        for step in z_steps:
            peer = lax.rem(z + step, nz)
            send(place, place, s_sem.at[h, peer], r_sem.at[h, z], row, 2 * peer + core)

    def found_z(h, panel, r_sem):
        for step in z_steps:
            peer = lax.rem(z + step, nz)
            arrive(solved.at[panel, peer, core, rows_of(h)], r_sem.at[h, peer])
        found = solved[panel, :, core, rows_of(h)]
        along_x[panel, x, :, rows_of(h)] = found
        along_y[panel, y, :, rows_of(h)] = found
        return found.reshape(nz * part, width)

    def gather_upper(h):
        source = loads_hbm.at[1, rows_of(h)]
        target = gathered.at[h, slot, core]
        for step in plane_steps:
            peer = beside(step)
            send(source, target, s_a.at[h, peer], r_a.at[h, slot, core], peer, 2 * z + parity)

        @pl.when(jnp.logical_not(holder))
        def _():
            send(source, target, s_a.at[h, row], r_a.at[h, slot, core], row, sibling)

    def multiply_upper(h):
        for block in range(nz):
            for source in (0, 1):
                @pl.when(jnp.logical_not(jnp.logical_and(2 * block + core == row, source == core)))
                def _():
                    arrive(gathered.at[h, block, source], r_a.at[h, block, source])
        left = jnp.concatenate([gathered[h, :, source].reshape(nz * part, width) for source in (0, 1)], axis=1)
        part_up[h] = product(halves(left), upper_diag).reshape(nz, part, width)
        scatter_z(h, part_up, land_up, s_b, r_b)

    def multiply_cross(h):
        upper = found_z(h, 1, r_c)
        part_cross[h] = product(halves(upper), cross_halves).reshape(nz, part, 2 * width)
        for step in range(nz):
            block = lax.rem(slot + nz // 2 + step, nz)
            owner = 2 * block + core

            @pl.when(owner != row)
            def _():
                send(part_cross.at[h, block], land_cross.at[h, row], s_d.at[h, block], r_d.at[h, row], owner, col)

    def reduce_cross(h):
        @pl.when(holder)
        def _():
            value = jnp.concatenate([loads[0, rows_of(h)], loads[1, rows_of(h)]], axis=1) - part_cross[h, slot]
            for step in plane_steps:
                peer = beside(step)
                arrive(land_cross.at[h, peer], r_d.at[h, peer])
                value = value - land_cross[h, peer]
            place = lower.at[h, slot]
            place[...] = value
            for step in plane_steps:
                peer = beside(step)
                send(place, place, s_e.at[h, peer], r_e.at[h, slot], peer, col)

    def multiply_lower(h):
        for block in range(nz):
            @pl.when(2 * block + core != row)
            def _():
                arrive(lower.at[h, block], r_e.at[h, block])
        part_low[h] = product(halves(lower[h].reshape(nz * part, 2 * width)), lower_diag).reshape(nz, part, width)
        scatter_z(h, part_low, land_low, s_f, r_f)

    def forward(h, panel):
        for step in x_steps[panel:]:
            peer = lax.rem(x + step, nx)
            place = along_x.at[panel, x, :, rows_of(h)]
            send(place, place, s_lx.at[h, panel, peer], r_lx.at[h, panel, x], y * nx + peer, col)
        for step in y_steps[panel:]:
            peer = lax.rem(y + step, ny)
            place = along_y.at[panel, y, :, rows_of(h)]
            send(place, place, s_ly.at[h, panel, peer], r_ly.at[h, panel, y], peer * nx + x, col)

    def deal(panel):
        for step in x_steps:
            peer = lax.rem(x + step, nx)
            send(
                coupling_hbm.at[panel, :, pl.ds(pl.multiple_of(peer * qx, qx), qx)], raw_x.at[core, panel, x],
                s_px.at[panel, peer], r_px.at[panel, x], y * nx + peer, col,
            )
        for step in y_steps:
            peer = lax.rem(y + step, ny)
            send(
                coupling_hbm.at[panel, :, pl.ds(pl.multiple_of(nx * qx + peer * qy, qy), qy)], raw_y.at[core, panel, y],
                s_py.at[panel, peer], r_py.at[panel, y], peer * nx + x, col,
            )

    def share_dealt(panel):
        for step in x_steps:
            peer = lax.rem(x + step, nx)
            arrive(raw_x.at[core, panel, peer], r_px.at[panel, peer])
        send(raw_x.at[core, panel], raw_x.at[core, panel], s_deal.at[panel, 0], r_deal.at[panel, 0], row, sibling)
        for step in y_steps:
            peer = lax.rem(y + step, ny)
            arrive(raw_y.at[core, panel, peer], r_py.at[panel, peer])
        send(raw_y.at[core, panel], raw_y.at[core, panel], s_deal.at[panel, 1], r_deal.at[panel, 1], row, sibling)

    def split_dealt(panel):
        arrive(raw_x.at[1 - core, panel], r_deal.at[panel, 0])
        arrive(raw_y.at[1 - core, panel], r_deal.at[panel, 1])
        for raw, high, low, groups in ((raw_x, high_x, low_x, nx), (raw_y, high_y, low_y, ny)):
            @pl.loop(0, 2 * groups)
            def _(index):
                owner, group = lax.div(index, groups), lax.rem(index, groups)
                start = pl.multiple_of((panel * groups + group) * width, width)
                block_high, block_low = halves(raw[owner, panel, group])
                high[owner, pl.ds(start, width)] = block_high
                low[owner, pl.ds(start, width)] = block_low

    send(diag_hbm, diag.at[core], s_swap.at[0], r_swap.at[0], row, sibling)
    gather_upper(0)
    gather_upper(1)
    send(cross_hbm, cross.at[core], s_swap.at[1], r_swap.at[1], row, sibling)
    send(loads_hbm.at[0], loads.at[core], s_swap.at[2], r_swap.at[2], row, sibling)

    own_copies[0].wait()
    arrive(diag.at[1 - core], r_swap.at[0])

    @pl.when(holder)
    def _():
        for copy in own_upper:
            copy.wait()

    upper_diag = halves(diag[:, 1].reshape(2 * width, width))
    multiply_upper(0)
    deal(1)
    multiply_upper(1)

    own_copies[1].wait()
    arrive(cross.at[1 - core], r_swap.at[1])
    cross_halves = halves(jnp.concatenate([cross[0], cross[1]], axis=1))
    for h in (0, 1):
        spread_z(h, 1, total_z(h, part_up, land_up, r_b), s_c, r_c)

    x_far, y_far = lax.rem(x + half, nx), lax.rem(y + half, ny)
    own_block = solved.at[1, z, core]
    send(own_block, along_x.at[1, x, z], s_far.at[0], r_far.at[0], y * nx + x_far, col)
    send(own_block, along_y.at[1, y, z], s_far.at[1], r_far.at[1], y_far * nx + x, col)

    own_copies[2].wait()
    arrive(loads.at[1 - core], r_swap.at[2])
    for h in (0, 1):
        multiply_cross(h)
    far_places = (along_x.at[1, x_far], along_y.at[1, y_far])
    for axis in (0, 1):
        place = far_places[axis].at[z]
        arrive(place, r_far.at[axis])
        for step in z_steps:
            peer = lax.rem(z + step, nz)
            send(place, place, s_fz.at[axis, peer], r_fz.at[axis, z], row, 2 * peer + core)
    for h in (0, 1):
        reduce_cross(h)
    deal(0)

    lower_diag = halves(diag[:, 0].reshape(2 * width, width))
    for h in (0, 1):
        multiply_lower(h)

    for h in (0, 1):
        forward(h, 1)
    send(solved.at[1, :, core], solved.at[1, :, core], s_out.at[1], r_out.at[1], row, sibling)

    own_copies[4].wait()
    own_copies[5].wait()
    for h in (0, 1):
        spread_z(h, 0, total_z(h, part_low, land_low, r_f), s_g, r_g)
    share_dealt(1)
    share_dealt(0)
    for h in (0, 1):
        found_z(h, 0, r_g)
        forward(h, 0)
    send(solved.at[0, :, core], solved.at[0, :, core], s_out.at[0], r_out.at[0], row, sibling)
    split_dealt(1)
    split_dealt(0)

    def await_solved(axis):
        along, me, size, steps, recv = (
            (along_x, x, nx, x_steps, r_lx), (along_y, y, ny, y_steps, r_ly)
        )[axis]
        for step in z_steps:
            peer = lax.rem(z + step, nz)
            arrive(far_places[axis].at[peer], r_fz.at[axis, peer])
        for h in (0, 1):
            for panel in (1, 0):
                for step in steps[panel:]:
                    peer = lax.rem(me + step, size)
                    arrive(along.at[panel, peer, :, rows_of(h)], recv.at[h, panel, peer])

    y_up, y_down = lax.rem(y + 1, ny), lax.rem(y + ny - 1, ny)
    x_up, x_down = lax.rem(x + 1, nx), lax.rem(x + nx - 1, nx)
    row_up, row_down = y_up * nx + x, y_down * nx + x
    side_up, side_down = y * nx + x_up, y * nx + x_down
    own_offset = lax.div(x, 2)
    up_offset, down_offset = lax.div(x_up, 2), lax.div(x_down, 2)
    first, last = pl.ds(0, half), pl.ds(half, half)
    bridge = jnp.logical_not(holder)

    def tile_over_y(peer, owner):
        left = halves(jnp.concatenate(
            [
                along_x[panel, group, pl.ds(peer * half, half)].reshape(half * height, width)
                for panel in (0, 1) for group in range(nx)
            ],
            axis=1,
        ))
        value = product(left, (high_x[owner], low_x[owner]))
        sum_x[peer, :, owner] = value.reshape(half, height, qx)

    def tile_over_x(offset, start, owner):
        left = halves(jnp.concatenate(
            [
                jnp.concatenate([along_y[panel, group, (start + part) * half + offset] for part in range(half)], axis=0)
                for panel in (0, 1) for group in range(ny)
            ],
            axis=1,
        ))
        value = product(left, (high_y[owner], low_y[owner]))
        sum_y[offset, pl.ds(start, half), owner] = value.reshape(half, height, qy)

    def early(owner):
        if owner == 0:
            await_solved(1)
        tile_over_x(jnp.where(holder, 1 - own_offset, up_offset), jnp.where(holder, 0, half), owner)

        @pl.when(holder)
        def _():
            send(sum_y.at[1 - own_offset, first, owner], relay_y.at[0, :, owner],
                 s_ry.at[owner, 0], r_ry.at[owner, 0], side_up, col)

        @pl.when(bridge)
        def _():
            send(sum_y.at[up_offset, last, owner], land_y.at[0, last, owner],
                 s_sy.at[owner, 0, 1], r_sy.at[owner, 0, 1], side_up, col)

        if owner == 0:
            await_solved(0)
        tile_over_y(y_far, owner)
        send(sum_x.at[y_far, 0, owner], relay_x.at[0, owner], s_rx.at[owner, 0], r_rx.at[owner, 0], row_up, col)
        send(sum_x.at[y_far, 1, owner], relay_x.at[1, owner], s_rx.at[owner, 1], r_rx.at[owner, 1], row_down, col)

        tile_over_x(jnp.where(holder, 1 - own_offset, down_offset), jnp.where(holder, half, 0), owner)

        @pl.when(holder)
        def _():
            send(sum_y.at[1 - own_offset, last, owner], relay_y.at[1, :, owner],
                 s_ry.at[owner, 1], r_ry.at[owner, 1], side_down, col)

        @pl.when(bridge)
        def _():
            send(sum_y.at[down_offset, first, owner], land_y.at[1, first, owner],
                 s_sy.at[owner, 1, 0], r_sy.at[owner, 1, 0], side_down, col)

        tile_over_y(y_up, owner)
        send(sum_x.at[y_up, 1, owner], land_x.at[0, 1, owner], s_sx.at[owner, 0, 1], r_sx.at[owner, 0, 1], row_up, col)
        tile_over_y(y_down, owner)
        send(sum_x.at[y_down, 0, owner], land_x.at[1, 0, owner], s_sx.at[owner, 1, 0], r_sx.at[owner, 1, 0], row_down, col)

    def late(owner):
        tile_over_x(jnp.where(holder, own_offset, up_offset), 0, owner)

        @pl.when(bridge)
        def _():
            arrive(relay_y.at[0, :, owner], r_ry.at[owner, 0])
            sum_y[up_offset, first, owner] = sum_y[up_offset, first, owner] + relay_y[0, :, owner]
            send(sum_y.at[up_offset, first, owner], land_y.at[0, first, owner],
                 s_sy.at[owner, 0, 0], r_sy.at[owner, 0, 0], side_up, col)

        arrive(relay_x.at[0, owner], r_rx.at[owner, 0])
        sum_x[y_up, 0, owner] = sum_x[y_up, 0, owner] + relay_x[0, owner]
        send(sum_x.at[y_up, 0, owner], land_x.at[0, 0, owner], s_sx.at[owner, 0, 0], r_sx.at[owner, 0, 0], row_up, col)
        arrive(relay_x.at[1, owner], r_rx.at[owner, 1])
        sum_x[y_down, 1, owner] = sum_x[y_down, 1, owner] + relay_x[1, owner]
        send(sum_x.at[y_down, 1, owner], land_x.at[1, 1, owner], s_sx.at[owner, 1, 1], r_sx.at[owner, 1, 1], row_down, col)

        tile_over_x(jnp.where(holder, own_offset, down_offset), half, owner)

        @pl.when(bridge)
        def _():
            arrive(relay_y.at[1, :, owner], r_ry.at[owner, 1])
            sum_y[down_offset, last, owner] = sum_y[down_offset, last, owner] + relay_y[1, :, owner]
            send(sum_y.at[down_offset, last, owner], land_y.at[1, last, owner],
                 s_sy.at[owner, 1, 1], r_sy.at[owner, 1, 1], side_down, col)

        tile_over_y(y, owner)

    def finish(owner):
        for offset in range(half):
            for side in (0, 1):
                arrive(land_x.at[side, offset, owner], r_sx.at[owner, side, offset])
            done_x[offset, owner] = sum_x[y, offset, owner] + land_x[0, offset, owner] + land_x[1, offset, owner]
            target = 2 * offset + core

            @pl.when(jnp.logical_not(jnp.logical_and(target == x, owner == core)))
            def _():
                send(
                    done_x.at[offset, owner], tile_x.at[x], s_tx.at[offset, owner], r_tx.at[x],
                    y * nx + target, 2 * z + owner,
                )

        @pl.when(holder)
        def _():
            for peer in range(ny):
                if peer % half == 0:
                    for side in (0, 1):
                        arrive(land_y.at[side, pl.ds(peer, half), owner], r_sy.at[owner, side, peer // half])
                done_y[peer, owner] = sum_y[own_offset, peer, owner] + land_y[0, peer, owner] + land_y[1, peer, owner]

                @pl.when(jnp.logical_not(jnp.logical_and(peer == y, owner == core)))
                def _():
                    send(
                        done_y.at[peer, owner], tile_y.at[y], s_ty.at[peer, owner], r_ty.at[y],
                        peer * nx + x, 2 * z + owner,
                    )

    early(0)
    late(0)
    early(1)
    finish(0)
    late(1)
    finish(1)
    own_copies[3].wait()

    @pl.when(holder)
    def _():
        tile_x[x] = done_x[own_offset, core]
        tile_y[y] = done_y[y, core]

    for group in range(nx):
        @pl.when(jnp.logical_not(jnp.logical_and(holder, group == x)))
        def _():
            arrive(tile_x.at[group], r_tx.at[group])

        columns = pl.ds(group * qx, qx)
        out[:, columns] = rest[:, columns] - tile_x[group]

    for group in range(ny):
        @pl.when(jnp.logical_not(jnp.logical_and(holder, group == y)))
        def _():
            arrive(tile_y.at[group], r_ty.at[group])

        columns = pl.ds(nx * qx + group * qy, qy)
        out[:, columns] = rest[:, columns] - tile_y[group]

    for panel in (0, 1):
        arrive(solved.at[panel, :, 1 - core], r_out.at[panel])

    sent(diag.at[core], s_swap.at[0])
    sent(cross.at[core], s_swap.at[1])
    sent(loads.at[core], s_swap.at[2])
    for panel in (0, 1):
        sent(solved.at[panel, :, core], s_out.at[panel])
    for panel in (0, 1):
        sent(raw_x.at[core, panel], s_deal.at[panel, 0])
        sent(raw_y.at[core, panel], s_deal.at[panel, 1])

    for h in (0, 1):
        @pl.loop(0, rows)
        def _(step):
            peer = lax.rem(row + step, rows)

            @pl.when(jnp.logical_or(step > 0, jnp.logical_not(holder)))
            def _():
                sent(gathered.at[0, 0, 0], s_a.at[h, peer])

            @pl.when(jnp.logical_and(step > 0, holder))
            def _():
                sent(lower.at[0, 0], s_e.at[h, peer])

        @pl.loop(1, nz)
        def _(step):
            peer = lax.rem(z + step, nz)
            for sem in (s_b, s_c, s_f, s_g):
                sent(part_up.at[0, 0], sem.at[h, peer])

        @pl.loop(0, nz)
        def _(block):
            @pl.when(2 * block + core != row)
            def _():
                sent(part_cross.at[0, 0], s_d.at[h, block])

        for panel in (0, 1):
            for step in x_steps[panel:]:
                sent(along_x.at[0, 0, :, rows_of(0)], s_lx.at[h, panel, lax.rem(x + step, nx)])
            for step in y_steps[panel:]:
                sent(along_y.at[0, 0, :, rows_of(0)], s_ly.at[h, panel, lax.rem(y + step, ny)])

    @pl.loop(1, nx)
    def _(step):
        peer = lax.rem(x + step, nx)
        for panel in (0, 1):
            sent(raw_x.at[core, panel, 0], s_px.at[panel, peer])

    @pl.loop(1, ny)
    def _(step):
        peer = lax.rem(y + step, ny)
        for panel in (0, 1):
            sent(raw_y.at[core, panel, 0], s_py.at[panel, peer])

    @pl.loop(0, half)
    def _(offset):
        target = 2 * offset + core
        for owner in (0, 1):
            @pl.when(jnp.logical_not(jnp.logical_and(target == x, owner == core)))
            def _():
                sent(done_x.at[0, 0], s_tx.at[offset, owner])

    for axis in (0, 1):
        sent(own_block, s_far.at[axis])
        for step in z_steps:
            sent(own_block, s_fz.at[axis, lax.rem(z + step, nz)])

    for owner in (0, 1):
        for side in (0, 1):
            sent(relay_x.at[0, 0], s_rx.at[owner, side])
            for piece in (0, 1):
                sent(land_x.at[0, 0, 0], s_sx.at[owner, side, piece])

                @pl.when(bridge)
                def _():
                    sent(land_y.at[0, first, 0], s_sy.at[owner, side, piece])

            @pl.when(holder)
            def _():
                sent(relay_y.at[0, :, 0], s_ry.at[owner, side])

    @pl.when(holder)
    def _():
        @pl.loop(0, ny)
        def _(peer):
            for owner in (0, 1):
                @pl.when(jnp.logical_not(jnp.logical_and(peer == y, owner == core)))
                def _():
                    sent(done_y.at[0, 0], s_ty.at[peer, owner])


def local(mesh, diag_inv, cross_block, coupling, panel_loads, rest_loads):
    rows, cols = mesh.shape["row"], mesh.shape["col"]
    nx = ny = math.isqrt(rows)
    nz, half = cols // 2, math.isqrt(rows) // 2
    _, height, width = panel_loads.shape
    span = rest_loads.shape[1]
    qx, qy = span // 2 // nx, span // 2 // ny
    f32, bf16 = jnp.float32, jnp.bfloat16
    vmem, dma = pltpu.VMEM, lambda *shape: pltpu.SemaphoreType.DMA(shape)
    block, piece = (height, width), (height // 2, width)
    whole = pl.BlockSpec(memory_space=pltpu.VMEM)
    solved, rest_updated = pl.pallas_call(
        functools.partial(solve_kernel, (rows, nx, ny, nz, height, width, qx, qy)),
        out_shape=(
            jax.ShapeDtypeStruct((2, nz, 2) + block, f32),
            jax.ShapeDtypeStruct((height, span), f32),
        ),
        in_specs=[pl.BlockSpec(memory_space=pltpu.HBM)] * 5,
        out_specs=(whole, whole),
        scratch_shapes=[
            vmem((2, 2, width, width), f32),
            vmem((2, width, width), f32),
            vmem((2,) + block, f32),
            vmem((height, span), f32),
            vmem((2, nz, 2) + piece, f32),
            vmem((2, nz) + piece, f32),
            vmem((2, nz) + piece, f32),
            vmem((2, nz, height // 2, 2 * width), f32),
            vmem((2, rows, height // 2, 2 * width), f32),
            vmem((2, nz, height // 2, 2 * width), f32),
            vmem((2, nz) + piece, f32),
            vmem((2, nz) + piece, f32),
            vmem((2, 2, nx, width, qx), f32),
            vmem((2, 2, ny, width, qy), f32),
            vmem((2, 2 * nx * width, qx), bf16),
            vmem((2, 2 * nx * width, qx), bf16),
            vmem((2, 2 * ny * width, qy), bf16),
            vmem((2, 2 * ny * width, qy), bf16),
            vmem((2, nx, nz) + block, f32),
            vmem((2, ny, nz) + block, f32),
            vmem((ny, half, 2, height, qx), f32),
            vmem((2, half, 2, height, qx), f32),
            vmem((2, 2, height, qx), f32),
            vmem((half, ny, 2, height, qy), f32),
            vmem((2, ny, 2, height, qy), f32),
            vmem((2, half, 2, height, qy), f32),
            vmem((half, 2, height, qx), f32),
            vmem((ny, 2, height, qy), f32),
            vmem((nx, height, qx), f32),
            vmem((ny, height, qy), f32),
            dma(8), dma(3), dma(3),
            dma(2, rows), dma(2, nz, 2),
            dma(2, nz), dma(2, nz), dma(2, nz), dma(2, nz),
            dma(2, nz), dma(2, rows), dma(2, rows), dma(2, nz),
            dma(2, nz), dma(2, nz), dma(2, nz), dma(2, nz),
            dma(2, nx), dma(2, nx), dma(2, ny), dma(2, ny), dma(2, 2), dma(2, 2),
            dma(2, 2, nx), dma(2, 2, nx), dma(2, 2, ny), dma(2, 2, ny),
            dma(2, 2, 2), dma(2, 2, 2), dma(2, 2, 2), dma(2, 2, 2), dma(2, 2), dma(2, 2), dma(2, 2), dma(2, 2),
            dma(2), dma(2), dma(2, nz), dma(2, nz),
            dma(half, 2), dma(nx), dma(ny, 2), dma(ny),
            dma(2), dma(2),
        ],
        compiler_params=pltpu.CompilerParams(
            collective_id=0, has_side_effects=True, vmem_limit_bytes=42 * 2**20
        ),
    )(*(pltpu.with_memory_space_constraint(arg, pltpu.HBM) for arg in (diag_inv, cross_block, coupling, panel_loads, rest_loads)))
    return solved.reshape(2, rows * height, width), rest_updated


def solution(mesh):
    in_specs = (
        P(None, "col", "row"),
        P("row", "col"),
        P(None, "row", "col"),
        P(None, "row", "col"),
        P("row", "col"),
    )
    out_specs = (P(None, None, "row"), P("row", "col"))
    return jax.shard_map(
        functools.partial(local, mesh), mesh=mesh, in_specs=in_specs, out_specs=out_specs, check_vma=False
    )
```

```python
import functools
import math

import jax
import jax.numpy as jnp
from jax import lax
from jax.experimental import pallas as pl
from jax.experimental.pallas import tpu as pltpu
from jax.sharding import PartitionSpec as P

MESH = pl.DeviceIdType.MESH


def halves(value):
    high = value.astype(jnp.bfloat16)
    low = (value - high.astype(jnp.float32)).astype(jnp.bfloat16)
    return high, low


def product(left_halves, right_halves):
    left_high, left_low = left_halves
    right_high, right_low = right_halves
    dot = functools.partial(jnp.dot, preferred_element_type=jnp.float32)
    rows = left_high.shape[0]
    both = dot(jnp.concatenate([left_high, left_low], axis=0), right_high)
    return both[:rows] + (both[rows:] + dot(left_high, right_low))


def farthest_first(size):
    return sorted(range(1, size), key=lambda step: -min(step, size - step))


def solve_kernel(
    dims,
    diag_hbm, cross_hbm, coupling_hbm, loads_hbm, rest_hbm,
    solved, out,
    diag, cross, loads, rest,
    gathered, part_up, land_up, part_cross, land_cross, lower, part_low, land_low,
    raw_x, raw_y, high_x, low_x, high_y, low_y,
    along_x, along_y, sum_x, land_x, relay_x, sum_y, land_y, relay_y, done_x, done_y, tile_x, tile_y,
    local_sem, s_swap, r_swap, s_a, r_a, s_b, r_b, s_c, r_c, s_d, r_d, s_e, r_e, s_f, r_f, s_g, r_g,
    s_px, r_px, s_py, r_py, s_deal, r_deal, s_lx, r_lx, s_ly, r_ly,
    s_sx, r_sx, s_sy, r_sy, s_rx, r_rx, s_ry, r_ry, s_far, r_far, s_fz, r_fz, s_tx, r_tx, s_ty, r_ty, s_out, r_out,
):
    rows, nx, ny, nz, height, width, qx, qy = dims
    half, part = nx // 2, height // 2
    x_steps, y_steps, z_steps = farthest_first(nx), farthest_first(ny), farthest_first(nz)
    plane_steps = sorted(
        ((dy, dx) for dy in range(ny) for dx in range(nx) if (dy, dx) != (0, 0)),
        key=lambda step: -min(step[0], ny - step[0]) - min(step[1], nx - step[1]),
    )
    row, col = lax.axis_index("row"), lax.axis_index("col")
    y, x = lax.div(row, nx), lax.rem(row, nx)
    z, core = lax.div(col, 2), lax.rem(col, 2)
    parity, slot = lax.rem(row, 2), lax.div(row, 2)
    holder = parity == core
    sibling = 2 * z + 1 - core

    def beside(step):
        return lax.rem(y + step[0], ny) * nx + lax.rem(x + step[1], nx)

    def send(source, target, send_sem, recv_sem, to_row, to_col):
        copy = pltpu.make_async_remote_copy(
            src_ref=source, dst_ref=target, send_sem=send_sem, recv_sem=recv_sem,
            device_id={"row": to_row, "col": to_col}, device_id_type=MESH,
        )
        copy.start()

    def arrive(place, recv_sem):
        pltpu.make_async_remote_copy(
            src_ref=place, dst_ref=place, send_sem=s_swap.at[0], recv_sem=recv_sem,
            device_id={"row": row, "col": sibling}, device_id_type=MESH,
        ).wait_recv()

    def sent(place, send_sem):
        pltpu.make_async_remote_copy(
            src_ref=place, dst_ref=place, send_sem=send_sem, recv_sem=r_swap.at[0],
            device_id={"row": row, "col": sibling}, device_id_type=MESH,
        ).wait_send()

    own_copies = [
        pltpu.make_async_copy(diag_hbm, diag.at[core], local_sem.at[0]),
        pltpu.make_async_copy(cross_hbm, cross.at[core], local_sem.at[1]),
        pltpu.make_async_copy(loads_hbm.at[0], loads.at[core], local_sem.at[2]),
        pltpu.make_async_copy(rest_hbm, rest, local_sem.at[3]),
        pltpu.make_async_copy(
            coupling_hbm.at[:, :, pl.ds(pl.multiple_of(x * qx, qx), qx)], raw_x.at[core, :, x], local_sem.at[4]
        ),
        pltpu.make_async_copy(
            coupling_hbm.at[:, :, pl.ds(pl.multiple_of(nx * qx + y * qy, qy), qy)], raw_y.at[core, :, y], local_sem.at[5]
        ),
    ]
    own_upper = [
        pltpu.make_async_copy(loads_hbm.at[1, pl.ds(h * part, part)], gathered.at[h, slot, core], local_sem.at[6 + h])
        for h in (0, 1)
    ]

    barrier = pltpu.get_barrier_semaphore()

    def greet(to_row, to_col):
        pl.semaphore_signal(barrier, inc=1, device_id={"row": to_row, "col": to_col}, device_id_type=MESH)

    for step in z_steps:
        greet(row, 2 * lax.rem(z + step, nz) + core)
    for step in plane_steps:
        greet(beside(step), col)
        greet(beside(step), sibling)
    greet(row, sibling)

    for copy in own_copies:
        copy.start()

    @pl.when(holder)
    def _():
        for copy in own_upper:
            copy.start()

    pl.semaphore_wait(barrier, 2 * rows - 1 + nz - 1)

    def rows_of(h):
        return pl.ds(h * part, part)

    def scatter_z(h, parts, landing, s_sem, r_sem):
        for step in z_steps:
            peer = lax.rem(z + step, nz)
            send(parts.at[h, peer], landing.at[h, z], s_sem.at[h, peer], r_sem.at[h, z], row, 2 * peer + core)

    def total_z(h, parts, landing, r_sem):
        value = parts[h, z]
        for step in z_steps:
            peer = lax.rem(z + step, nz)
            arrive(landing.at[h, peer], r_sem.at[h, peer])
            value = value + landing[h, peer]
        return value

    def spread_z(h, panel, value, s_sem, r_sem):
        place = solved.at[panel, z, core, rows_of(h)]
        place[...] = value
        for step in z_steps:
            peer = lax.rem(z + step, nz)
            send(place, place, s_sem.at[h, peer], r_sem.at[h, z], row, 2 * peer + core)

    def found_z(h, panel, r_sem):
        for step in z_steps:
            peer = lax.rem(z + step, nz)
            arrive(solved.at[panel, peer, core, rows_of(h)], r_sem.at[h, peer])
        found = solved[panel, :, core, rows_of(h)]
        along_x[panel, x, :, rows_of(h)] = found
        along_y[panel, y, :, rows_of(h)] = found
        return found.reshape(nz * part, width)

    def gather_upper(h):
        source = loads_hbm.at[1, rows_of(h)]
        target = gathered.at[h, slot, core]
        for step in plane_steps:
            peer = beside(step)
            send(source, target, s_a.at[h, peer], r_a.at[h, slot, core], peer, 2 * z + parity)

        @pl.when(jnp.logical_not(holder))
        def _():
            send(source, target, s_a.at[h, row], r_a.at[h, slot, core], row, sibling)

    def multiply_upper(h):
        for block in range(nz):
            for source in (0, 1):
                @pl.when(jnp.logical_not(jnp.logical_and(2 * block + core == row, source == core)))
                def _():
                    arrive(gathered.at[h, block, source], r_a.at[h, block, source])
        left = jnp.concatenate([gathered[h, :, source].reshape(nz * part, width) for source in (0, 1)], axis=1)
        part_up[h] = product(halves(left), upper_diag).reshape(nz, part, width)
        scatter_z(h, part_up, land_up, s_b, r_b)

    def multiply_cross(h):
        upper = found_z(h, 1, r_c)
        part_cross[h] = product(halves(upper), cross_halves).reshape(nz, part, 2 * width)
        for step in range(nz):
            block = lax.rem(slot + nz // 2 + step, nz)
            owner = 2 * block + core

            @pl.when(owner != row)
            def _():
                send(part_cross.at[h, block], land_cross.at[h, row], s_d.at[h, block], r_d.at[h, row], owner, col)

    def reduce_cross(h):
        @pl.when(holder)
        def _():
            value = jnp.concatenate([loads[0, rows_of(h)], loads[1, rows_of(h)]], axis=1) - part_cross[h, slot]
            for step in plane_steps:
                peer = beside(step)
                arrive(land_cross.at[h, peer], r_d.at[h, peer])
                value = value - land_cross[h, peer]
            place = lower.at[h, slot]
            place[...] = value
            for step in plane_steps:
                peer = beside(step)
                send(place, place, s_e.at[h, peer], r_e.at[h, slot], peer, col)

    def multiply_lower(h):
        for block in range(nz):
            @pl.when(2 * block + core != row)
            def _():
                arrive(lower.at[h, block], r_e.at[h, block])
        part_low[h] = product(halves(lower[h].reshape(nz * part, 2 * width)), lower_diag).reshape(nz, part, width)
        scatter_z(h, part_low, land_low, s_f, r_f)

    def forward(h, panel):
        for step in x_steps[panel:]:
            peer = lax.rem(x + step, nx)
            place = along_x.at[panel, x, :, rows_of(h)]
            send(place, place, s_lx.at[h, panel, peer], r_lx.at[h, panel, x], y * nx + peer, col)
        for step in y_steps[panel:]:
            peer = lax.rem(y + step, ny)
            place = along_y.at[panel, y, :, rows_of(h)]
            send(place, place, s_ly.at[h, panel, peer], r_ly.at[h, panel, y], peer * nx + x, col)

    def deal(panel):
        for step in x_steps:
            peer = lax.rem(x + step, nx)
            send(
                coupling_hbm.at[panel, :, pl.ds(pl.multiple_of(peer * qx, qx), qx)], raw_x.at[core, panel, x],
                s_px.at[panel, peer], r_px.at[panel, x], y * nx + peer, col,
            )
        for step in y_steps:
            peer = lax.rem(y + step, ny)
            send(
                coupling_hbm.at[panel, :, pl.ds(pl.multiple_of(nx * qx + peer * qy, qy), qy)], raw_y.at[core, panel, y],
                s_py.at[panel, peer], r_py.at[panel, y], peer * nx + x, col,
            )

    def share_dealt(panel):
        for step in x_steps:
            peer = lax.rem(x + step, nx)
            arrive(raw_x.at[core, panel, peer], r_px.at[panel, peer])
        send(raw_x.at[core, panel], raw_x.at[core, panel], s_deal.at[panel, 0], r_deal.at[panel, 0], row, sibling)
        for step in y_steps:
            peer = lax.rem(y + step, ny)
            arrive(raw_y.at[core, panel, peer], r_py.at[panel, peer])
        send(raw_y.at[core, panel], raw_y.at[core, panel], s_deal.at[panel, 1], r_deal.at[panel, 1], row, sibling)

    def split_dealt(panel):
        arrive(raw_x.at[1 - core, panel], r_deal.at[panel, 0])
        arrive(raw_y.at[1 - core, panel], r_deal.at[panel, 1])
        for raw, high, low, groups in ((raw_x, high_x, low_x, nx), (raw_y, high_y, low_y, ny)):
            @pl.loop(0, 2 * groups)
            def _(index):
                owner, group = lax.div(index, groups), lax.rem(index, groups)
                start = pl.multiple_of((panel * groups + group) * width, width)
                block_high, block_low = halves(raw[owner, panel, group])
                high[owner, pl.ds(start, width)] = block_high
                low[owner, pl.ds(start, width)] = block_low

    send(diag_hbm, diag.at[core], s_swap.at[0], r_swap.at[0], row, sibling)
    gather_upper(0)
    gather_upper(1)
    send(cross_hbm, cross.at[core], s_swap.at[1], r_swap.at[1], row, sibling)
    send(loads_hbm.at[0], loads.at[core], s_swap.at[2], r_swap.at[2], row, sibling)

    own_copies[0].wait()
    arrive(diag.at[1 - core], r_swap.at[0])

    @pl.when(holder)
    def _():
        for copy in own_upper:
            copy.wait()

    upper_diag = halves(diag[:, 1].reshape(2 * width, width))
    multiply_upper(0)
    deal(1)
    multiply_upper(1)

    own_copies[1].wait()
    arrive(cross.at[1 - core], r_swap.at[1])
    cross_halves = halves(jnp.concatenate([cross[0], cross[1]], axis=1))
    for h in (0, 1):
        spread_z(h, 1, total_z(h, part_up, land_up, r_b), s_c, r_c)

    x_far, y_far = lax.rem(x + half, nx), lax.rem(y + half, ny)
    own_block = solved.at[1, z, core]
    send(own_block, along_x.at[1, x, z], s_far.at[0], r_far.at[0], y * nx + x_far, col)
    send(own_block, along_y.at[1, y, z], s_far.at[1], r_far.at[1], y_far * nx + x, col)

    own_copies[2].wait()
    arrive(loads.at[1 - core], r_swap.at[2])
    for h in (0, 1):
        multiply_cross(h)
    far_places = (along_x.at[1, x_far], along_y.at[1, y_far])
    for axis in (0, 1):
        place = far_places[axis].at[z]
        arrive(place, r_far.at[axis])
        for step in z_steps:
            peer = lax.rem(z + step, nz)
            send(place, place, s_fz.at[axis, peer], r_fz.at[axis, z], row, 2 * peer + core)
    for h in (0, 1):
        reduce_cross(h)
    deal(0)

    lower_diag = halves(diag[:, 0].reshape(2 * width, width))
    for h in (0, 1):
        multiply_lower(h)

    for h in (0, 1):
        forward(h, 1)
    send(solved.at[1, :, core], solved.at[1, :, core], s_out.at[1], r_out.at[1], row, sibling)

    own_copies[4].wait()
    own_copies[5].wait()
    for h in (0, 1):
        spread_z(h, 0, total_z(h, part_low, land_low, r_f), s_g, r_g)
    share_dealt(1)
    share_dealt(0)
    for h in (0, 1):
        found_z(h, 0, r_g)
        forward(h, 0)
    send(solved.at[0, :, core], solved.at[0, :, core], s_out.at[0], r_out.at[0], row, sibling)
    split_dealt(1)
    split_dealt(0)

    def await_solved(axis):
        along, me, size, steps, recv = (
            (along_x, x, nx, x_steps, r_lx), (along_y, y, ny, y_steps, r_ly)
        )[axis]
        for step in z_steps:
            peer = lax.rem(z + step, nz)
            arrive(far_places[axis].at[peer], r_fz.at[axis, peer])
        for h in (0, 1):
            for panel in (1, 0):
                for step in steps[panel:]:
                    peer = lax.rem(me + step, size)
                    arrive(along.at[panel, peer, :, rows_of(h)], recv.at[h, panel, peer])

    y_up, y_down = lax.rem(y + 1, ny), lax.rem(y + ny - 1, ny)
    x_up, x_down = lax.rem(x + 1, nx), lax.rem(x + nx - 1, nx)
    row_up, row_down = y_up * nx + x, y_down * nx + x
    side_up, side_down = y * nx + x_up, y * nx + x_down
    own_offset = lax.div(x, 2)
    up_offset, down_offset = lax.div(x_up, 2), lax.div(x_down, 2)
    first, last = pl.ds(0, half), pl.ds(half, half)
    bridge = jnp.logical_not(holder)

    def tile_over_y(peer, owner):
        left = halves(jnp.concatenate(
            [
                along_x[panel, group, pl.ds(peer * half, half)].reshape(half * height, width)
                for panel in (0, 1) for group in range(nx)
            ],
            axis=1,
        ))
        value = product(left, (high_x[owner], low_x[owner]))
        sum_x[peer, :, owner] = value.reshape(half, height, qx)

    def tile_over_x(offset, start, owner):
        left = halves(jnp.concatenate(
            [
                jnp.concatenate([along_y[panel, group, (start + part) * half + offset] for part in range(half)], axis=0)
                for panel in (0, 1) for group in range(ny)
            ],
            axis=1,
        ))
        value = product(left, (high_y[owner], low_y[owner]))
        sum_y[offset, pl.ds(start, half), owner] = value.reshape(half, height, qy)

    def early(owner):
        if owner == 0:
            await_solved(1)
        tile_over_x(jnp.where(holder, 1 - own_offset, up_offset), jnp.where(holder, 0, half), owner)

        @pl.when(holder)
        def _():
            send(sum_y.at[1 - own_offset, first, owner], relay_y.at[0, :, owner],
                 s_ry.at[owner, 0], r_ry.at[owner, 0], side_up, col)

        @pl.when(bridge)
        def _():
            send(sum_y.at[up_offset, last, owner], land_y.at[0, last, owner],
                 s_sy.at[owner, 0, 1], r_sy.at[owner, 0, 1], side_up, col)

        if owner == 0:
            await_solved(0)
        tile_over_y(y_far, owner)
        send(sum_x.at[y_far, 0, owner], relay_x.at[0, owner], s_rx.at[owner, 0], r_rx.at[owner, 0], row_up, col)
        send(sum_x.at[y_far, 1, owner], relay_x.at[1, owner], s_rx.at[owner, 1], r_rx.at[owner, 1], row_down, col)

        tile_over_x(jnp.where(holder, 1 - own_offset, down_offset), jnp.where(holder, half, 0), owner)

        @pl.when(holder)
        def _():
            send(sum_y.at[1 - own_offset, last, owner], relay_y.at[1, :, owner],
                 s_ry.at[owner, 1], r_ry.at[owner, 1], side_down, col)

        @pl.when(bridge)
        def _():
            send(sum_y.at[down_offset, first, owner], land_y.at[1, first, owner],
                 s_sy.at[owner, 1, 0], r_sy.at[owner, 1, 0], side_down, col)

        tile_over_y(y_up, owner)
        send(sum_x.at[y_up, 1, owner], land_x.at[0, 1, owner], s_sx.at[owner, 0, 1], r_sx.at[owner, 0, 1], row_up, col)
        tile_over_y(y_down, owner)
        send(sum_x.at[y_down, 0, owner], land_x.at[1, 0, owner], s_sx.at[owner, 1, 0], r_sx.at[owner, 1, 0], row_down, col)

    def late(owner):
        tile_over_x(jnp.where(holder, own_offset, up_offset), 0, owner)

        @pl.when(bridge)
        def _():
            arrive(relay_y.at[0, :, owner], r_ry.at[owner, 0])
            sum_y[up_offset, first, owner] = sum_y[up_offset, first, owner] + relay_y[0, :, owner]
            send(sum_y.at[up_offset, first, owner], land_y.at[0, first, owner],
                 s_sy.at[owner, 0, 0], r_sy.at[owner, 0, 0], side_up, col)

        arrive(relay_x.at[0, owner], r_rx.at[owner, 0])
        sum_x[y_up, 0, owner] = sum_x[y_up, 0, owner] + relay_x[0, owner]
        send(sum_x.at[y_up, 0, owner], land_x.at[0, 0, owner], s_sx.at[owner, 0, 0], r_sx.at[owner, 0, 0], row_up, col)
        arrive(relay_x.at[1, owner], r_rx.at[owner, 1])
        sum_x[y_down, 1, owner] = sum_x[y_down, 1, owner] + relay_x[1, owner]
        send(sum_x.at[y_down, 1, owner], land_x.at[1, 1, owner], s_sx.at[owner, 1, 1], r_sx.at[owner, 1, 1], row_down, col)

        tile_over_x(jnp.where(holder, own_offset, down_offset), half, owner)

        @pl.when(bridge)
        def _():
            arrive(relay_y.at[1, :, owner], r_ry.at[owner, 1])
            sum_y[down_offset, last, owner] = sum_y[down_offset, last, owner] + relay_y[1, :, owner]
            send(sum_y.at[down_offset, last, owner], land_y.at[1, last, owner],
                 s_sy.at[owner, 1, 1], r_sy.at[owner, 1, 1], side_down, col)

        tile_over_y(y, owner)

    def finish(owner):
        for offset in range(half):
            for side in (0, 1):
                arrive(land_x.at[side, offset, owner], r_sx.at[owner, side, offset])
            done_x[offset, owner] = sum_x[y, offset, owner] + land_x[0, offset, owner] + land_x[1, offset, owner]
            target = 2 * offset + core

            @pl.when(jnp.logical_not(jnp.logical_and(target == x, owner == core)))
            def _():
                send(
                    done_x.at[offset, owner], tile_x.at[x], s_tx.at[offset, owner], r_tx.at[x],
                    y * nx + target, 2 * z + owner,
                )

        @pl.when(holder)
        def _():
            for peer in range(ny):
                if peer % half == 0:
                    for side in (0, 1):
                        arrive(land_y.at[side, pl.ds(peer, half), owner], r_sy.at[owner, side, peer // half])
                done_y[peer, owner] = sum_y[own_offset, peer, owner] + land_y[0, peer, owner] + land_y[1, peer, owner]

                @pl.when(jnp.logical_not(jnp.logical_and(peer == y, owner == core)))
                def _():
                    send(
                        done_y.at[peer, owner], tile_y.at[y], s_ty.at[peer, owner], r_ty.at[y],
                        peer * nx + x, 2 * z + owner,
                    )

    early(0)
    late(0)
    early(1)
    finish(0)
    late(1)
    finish(1)
    own_copies[3].wait()

    @pl.when(holder)
    def _():
        tile_x[x] = done_x[own_offset, core]
        tile_y[y] = done_y[y, core]

    for group in range(nx):
        @pl.when(jnp.logical_not(jnp.logical_and(holder, group == x)))
        def _():
            arrive(tile_x.at[group], r_tx.at[group])

        columns = pl.ds(group * qx, qx)
        out[:, columns] = rest[:, columns] - tile_x[group]

    for group in range(ny):
        @pl.when(jnp.logical_not(jnp.logical_and(holder, group == y)))
        def _():
            arrive(tile_y.at[group], r_ty.at[group])

        columns = pl.ds(nx * qx + group * qy, qy)
        out[:, columns] = rest[:, columns] - tile_y[group]

    for panel in (0, 1):
        arrive(solved.at[panel, :, 1 - core], r_out.at[panel])

    sent(diag.at[core], s_swap.at[0])
    sent(cross.at[core], s_swap.at[1])
    sent(loads.at[core], s_swap.at[2])
    for panel in (0, 1):
        sent(solved.at[panel, :, core], s_out.at[panel])
    for panel in (0, 1):
        sent(raw_x.at[core, panel], s_deal.at[panel, 0])
        sent(raw_y.at[core, panel], s_deal.at[panel, 1])

    for h in (0, 1):
        @pl.loop(0, rows)
        def _(step):
            peer = lax.rem(row + step, rows)

            @pl.when(jnp.logical_or(step > 0, jnp.logical_not(holder)))
            def _():
                sent(gathered.at[0, 0, 0], s_a.at[h, peer])

            @pl.when(jnp.logical_and(step > 0, holder))
            def _():
                sent(lower.at[0, 0], s_e.at[h, peer])

        @pl.loop(1, nz)
        def _(step):
            peer = lax.rem(z + step, nz)
            for sem in (s_b, s_c, s_f, s_g):
                sent(part_up.at[0, 0], sem.at[h, peer])

        @pl.loop(0, nz)
        def _(block):
            @pl.when(2 * block + core != row)
            def _():
                sent(part_cross.at[0, 0], s_d.at[h, block])

        for panel in (0, 1):
            for step in x_steps[panel:]:
                sent(along_x.at[0, 0, :, rows_of(0)], s_lx.at[h, panel, lax.rem(x + step, nx)])
            for step in y_steps[panel:]:
                sent(along_y.at[0, 0, :, rows_of(0)], s_ly.at[h, panel, lax.rem(y + step, ny)])

    @pl.loop(1, nx)
    def _(step):
        peer = lax.rem(x + step, nx)
        for panel in (0, 1):
            sent(raw_x.at[core, panel, 0], s_px.at[panel, peer])

    @pl.loop(1, ny)
    def _(step):
        peer = lax.rem(y + step, ny)
        for panel in (0, 1):
            sent(raw_y.at[core, panel, 0], s_py.at[panel, peer])

    @pl.loop(0, half)
    def _(offset):
        target = 2 * offset + core
        for owner in (0, 1):
            @pl.when(jnp.logical_not(jnp.logical_and(target == x, owner == core)))
            def _():
                sent(done_x.at[0, 0], s_tx.at[offset, owner])

    for axis in (0, 1):
        sent(own_block, s_far.at[axis])
        for step in z_steps:
            sent(own_block, s_fz.at[axis, lax.rem(z + step, nz)])

    for owner in (0, 1):
        for side in (0, 1):
            sent(relay_x.at[0, 0], s_rx.at[owner, side])
            for piece in (0, 1):
                sent(land_x.at[0, 0, 0], s_sx.at[owner, side, piece])

                @pl.when(bridge)
                def _():
                    sent(land_y.at[0, first, 0], s_sy.at[owner, side, piece])

            @pl.when(holder)
            def _():
                sent(relay_y.at[0, :, 0], s_ry.at[owner, side])

    @pl.when(holder)
    def _():
        @pl.loop(0, ny)
        def _(peer):
            for owner in (0, 1):
                @pl.when(jnp.logical_not(jnp.logical_and(peer == y, owner == core)))
                def _():
                    sent(done_y.at[0, 0], s_ty.at[peer, owner])


def local(mesh, diag_inv, cross_block, coupling, panel_loads, rest_loads):
    rows, cols = mesh.shape["row"], mesh.shape["col"]
    nx = ny = math.isqrt(rows)
    nz, half = cols // 2, math.isqrt(rows) // 2
    _, height, width = panel_loads.shape
    span = rest_loads.shape[1]
    qx, qy = span // 2 // nx, span // 2 // ny
    f32, bf16 = jnp.float32, jnp.bfloat16
    vmem, dma = pltpu.VMEM, lambda *shape: pltpu.SemaphoreType.DMA(shape)
    block, piece = (height, width), (height // 2, width)
    whole = pl.BlockSpec(memory_space=pltpu.VMEM)
    solved, rest_updated = pl.pallas_call(
        functools.partial(solve_kernel, (rows, nx, ny, nz, height, width, qx, qy)),
        out_shape=(
            jax.ShapeDtypeStruct((2, nz, 2) + block, f32),
            jax.ShapeDtypeStruct((height, span), f32),
        ),
        in_specs=[pl.BlockSpec(memory_space=pltpu.HBM)] * 5,
        out_specs=(whole, whole),
        scratch_shapes=[
            vmem((2, 2, width, width), f32),
            vmem((2, width, width), f32),
            vmem((2,) + block, f32),
            vmem((height, span), f32),
            vmem((2, nz, 2) + piece, f32),
            vmem((2, nz) + piece, f32),
            vmem((2, nz) + piece, f32),
            vmem((2, nz, height // 2, 2 * width), f32),
            vmem((2, rows, height // 2, 2 * width), f32),
            vmem((2, nz, height // 2, 2 * width), f32),
            vmem((2, nz) + piece, f32),
            vmem((2, nz) + piece, f32),
            vmem((2, 2, nx, width, qx), f32),
            vmem((2, 2, ny, width, qy), f32),
            vmem((2, 2 * nx * width, qx), bf16),
            vmem((2, 2 * nx * width, qx), bf16),
            vmem((2, 2 * ny * width, qy), bf16),
            vmem((2, 2 * ny * width, qy), bf16),
            vmem((2, nx, nz) + block, f32),
            vmem((2, ny, nz) + block, f32),
            vmem((ny, half, 2, height, qx), f32),
            vmem((2, half, 2, height, qx), f32),
            vmem((2, 2, height, qx), f32),
            vmem((half, ny, 2, height, qy), f32),
            vmem((2, ny, 2, height, qy), f32),
            vmem((2, half, 2, height, qy), f32),
            vmem((half, 2, height, qx), f32),
            vmem((ny, 2, height, qy), f32),
            vmem((nx, height, qx), f32),
            vmem((ny, height, qy), f32),
            dma(8), dma(3), dma(3),
            dma(2, rows), dma(2, nz, 2),
            dma(2, nz), dma(2, nz), dma(2, nz), dma(2, nz),
            dma(2, nz), dma(2, rows), dma(2, rows), dma(2, nz),
            dma(2, nz), dma(2, nz), dma(2, nz), dma(2, nz),
            dma(2, nx), dma(2, nx), dma(2, ny), dma(2, ny), dma(2, 2), dma(2, 2),
            dma(2, 2, nx), dma(2, 2, nx), dma(2, 2, ny), dma(2, 2, ny),
            dma(2, 2, 2), dma(2, 2, 2), dma(2, 2, 2), dma(2, 2, 2), dma(2, 2), dma(2, 2), dma(2, 2), dma(2, 2),
            dma(2), dma(2), dma(2, nz), dma(2, nz),
            dma(half, 2), dma(nx), dma(ny, 2), dma(ny),
            dma(2), dma(2),
        ],
        compiler_params=pltpu.CompilerParams(
            collective_id=0, has_side_effects=True, vmem_limit_bytes=42 * 2**20
        ),
    )(*(pltpu.with_memory_space_constraint(arg, pltpu.HBM) for arg in (diag_inv, cross_block, coupling, panel_loads, rest_loads)))
    return solved.reshape(2, rows * height, width), rest_updated


def solution(mesh):
    in_specs = (
        P(None, "col", "row"),
        P("row", "col"),
        P(None, "row", "col"),
        P(None, "row", "col"),
        P("row", "col"),
    )
    out_specs = (P(None, None, "row"), P("row", "col"))
    return jax.shard_map(
        functools.partial(local, mesh), mesh=mesh, in_specs=in_specs, out_specs=out_specs, check_vma=False
    )
```
